256 devices in a mesh: row: 8 (over x_hi, y), col: 32 (over x_lo, z, core).
Axes of the slice: x: 4 (x_hi: 2, x_lo: 2; x = x_hi * 2 + x_lo), y: 4, z: 8, core: 2. Of those that a mesh axis runs over, the one named last changes fastest.
Arguments:
- object_slices: float32 [2, 2, 4096, 8192], P(None, None, 'row', 'col'), may hold values from -5 to 5
- probe_field: float32 [2, 256, 256], replicated, may hold values from -6 to 6
- scan_offsets: int32 [8, 32, 2, 4], P('row', 'col'), may hold values from 0 to 7936, as said below
- scan_count: int32 [8, 32], P('row', 'col'), may hold values from 2 to 4, as said below
- measured: float32 [8, 32, 4, 256, 256], P('row', 'col'), may hold values from 0.2 to 2
Outputs:
- object_grad: float32 [2, 2, 4096, 8192], P(None, None, 'row', 'col')
- probe_grad: float32 [2, 256, 256], replicated
The draws below stay inside these ranges and needn't reach their ends.
Inputs may be any that keep to these rules, and one draw needn't show every extreme that they name: `scan_offsets`: for every tile and slot, the offsets are a window's first row and first column in global pixels; the window's centre (first row + 128, first column + 128) lies in that tile, and the whole window of 256 x 256 pixels lies inside the object. Slots at or beyond the tile's count hold offsets of the same kind and are not scanned. `scan_count`: some tile has all 4 slots scanned.
All inputs are finite; a program needn't handle non-finite values.
Results may differ from the reference program's by a relative error of at most 0.0003.
Values sent between devices are 32-bit elements; how exact they have to be, the bound alone decides.
A program may use at most 128 MiB of HBM per device.

```python
import math
import jax
import jax.numpy as jnp
from jax import lax

W = 256
LAYERS = 2
TH = 512
TW = 256
SLOTS = 4
NH = 4096
NW = 8192
POSITIONS = 1024
N_ROW = 8
N_COL = 32


def draw_scan_offsets(key, part):
    row_key = jax.random.fold_in(key, 11)
    col_key = jax.random.fold_in(key, 12)
    half = W // 2
    tile_rows = jnp.arange(N_ROW, dtype=jnp.int32)
    tile_cols = jnp.arange(N_COL, dtype=jnp.int32)
    row_local = jax.random.randint(row_key, (N_ROW, N_COL, SLOTS), 0, TH) - half
    col_local = jax.random.randint(col_key, (N_ROW, N_COL, SLOTS), 0, TW) - half
    row_local = row_local.at[0, :, 0].set(-half).at[N_ROW - 1, :, 1].set(TH - half - 1)
    col_local = col_local.at[:, 0, 0].set(-half).at[:, N_COL - 1, 1].set(TW - half - 1)
    row_global = jnp.clip(row_local + tile_rows[:, None, None] * TH, 0, NH - W)
    col_global = jnp.clip(col_local + tile_cols[None, :, None] * TW, 0, NW - W)
    return jnp.stack([row_global, col_global], axis=2).astype(jnp.int32)


def draw_scan_count(key, part):
    count_key = jax.random.fold_in(key, 21)
    counts = jax.random.randint(count_key, (N_ROW * N_COL,), 2, SLOTS + 1)
    counts = counts.at[0].set(2).at[N_ROW * N_COL - 1].set(SLOTS)
    return counts.reshape(N_ROW, N_COL).astype(jnp.int32)


def steps_of(stream_key, dims, pieces, least, largest):
    def one(dim, parts):
        steps = jax.random.uniform(jax.random.fold_in(jax.random.fold_in(stream_key, 6), dim), (parts,), jnp.float32, least / len(pieces), largest / len(pieces))
        return jnp.repeat(jnp.exp(steps), dims[dim] // parts).reshape((-1,) + (1,) * (len(dims) - dim - 1))

    gain = one(*pieces[0])
    for cut in pieces[1:]:
        gain = gain * one(*cut)
    return gain


def noise(rng, dims, width, most, cuts=(), kind=jnp.bfloat16):
    entries = width * jax.random.normal(rng, dims, jnp.float32)
    if cuts:
        entries = entries * steps_of(rng, dims, cuts, -0.22, 0.18)
    return jnp.clip(entries, -most, most).astype(kind)


def setup_inputs(seed: int = 0) -> dict:
    splits = jax.random.split(jax.random.key(seed), 6)
    object_slices = noise(splits[0], (LAYERS, 2, NH, NW), 0.7, 5.0, ((2, 8), (3, 32)), jnp.float32)
    probe_field = noise(splits[1], (2, W, W), 1.0, 6.0, (), jnp.float32)
    scan_offsets = draw_scan_offsets(jax.random.fold_in(splits[5], 71), 0)
    scan_count = draw_scan_count(jax.random.fold_in(splits[5], 71), 0)
    measured = jnp.clip(0.2 + 1.8 * jax.random.uniform(splits[4], (N_ROW, N_COL, SLOTS, W, W), jnp.float32) ** steps_of(splits[4], (N_ROW, N_COL, SLOTS, W, W), ((0, 8), (1, 32)), -0.2, 0.2), 0.2, 2.0)
    return {"object_slices": object_slices, "probe_field": probe_field, "scan_offsets": scan_offsets, "scan_count": scan_count, "measured": measured}


DEFOCUS = 0.3
FLOOR = 0.5

def dft_tables(window):
    indices = jnp.arange(window, dtype=jnp.int32)
    product = indices[:, None] * indices[None, :] % window
    angles = product.astype(jnp.float32) * (-2.0 * math.pi / window)
    norm_scale = 1.0 / math.sqrt(window)
    return (jnp.cos(angles) * norm_scale, jnp.sin(angles) * norm_scale)

def transfer_tables(window):
    indices = jnp.arange(window, dtype=jnp.int32)
    frequency = (indices + window // 2) % window - window // 2
    radius = frequency[:, None] * frequency[:, None] + frequency[None, :] * frequency[None, :]
    phases = radius.astype(jnp.float32) * (-math.pi * DEFOCUS / window)
    return (jnp.cos(phases), jnp.sin(phases))

def transform(x_re, x_im, c_re, c_im):
    highest = lax.Precision.HIGHEST
    y_re = jnp.einsum('jk,skl->sjl', c_re, x_re, precision=highest) - jnp.einsum('jk,skl->sjl', c_im, x_im, precision=highest)
    y_im = jnp.einsum('jk,skl->sjl', c_re, x_im, precision=highest) + jnp.einsum('jk,skl->sjl', c_im, x_re, precision=highest)
    z_re = jnp.einsum('sjk,kl->sjl', y_re, c_re, precision=highest) - jnp.einsum('sjk,kl->sjl', y_im, c_im, precision=highest)
    z_im = jnp.einsum('sjk,kl->sjl', y_re, c_im, precision=highest) + jnp.einsum('sjk,kl->sjl', y_im, c_re, precision=highest)
    return (z_re, z_im)

def propagate(x_re, x_im, tables, conjugate):
    c_re, c_im, h_re, h_im = tables
    if conjugate:
        h_im = -h_im
    f_re, f_im = transform(x_re, x_im, c_re, c_im)
    m_re = h_re * f_re - h_im * f_im
    m_im = h_re * f_im + h_im * f_re
    return transform(m_re, m_im, c_re, -c_im)

def slot_gradients(patches, probe_field, amplitudes, live_mask):
    layers = patches.shape[1]
    window = probe_field.shape[1]
    c_re, c_im = dft_tables(window)
    h_re, h_im = transfer_tables(window)
    tables = (c_re, c_im, h_re, h_im)
    cur_re = jnp.broadcast_to(probe_field[0], patches[:, 0, 0].shape)
    cur_im = jnp.broadcast_to(probe_field[1], patches[:, 0, 0].shape)
    saved = []
    for layer in range(layers):
        t_re = patches[:, layer, 0]
        t_im = patches[:, layer, 1]
        saved.append((cur_re, cur_im))
        e_re = t_re * cur_re - t_im * cur_im
        e_im = t_re * cur_im + t_im * cur_re
        if layer < layers - 1:
            cur_re, cur_im = propagate(e_re, e_im, tables, False)
    far_re, far_im = transform(e_re, e_im, c_re, c_im)
    magnitude = jnp.sqrt(far_re * far_re + far_im * far_im)
    weight = live_mask[:, None, None] * (1.0 - amplitudes / jnp.maximum(magnitude, FLOOR))
    back_re, back_im = transform(weight * far_re, weight * far_im, c_re, -c_im)
    layer_grads = []
    for layer in range(layers - 1, -1, -1):
        psi_re, psi_im = saved[layer]
        t_re = patches[:, layer, 0]
        t_im = patches[:, layer, 1]
        grad_re = psi_re * back_re + psi_im * back_im
        grad_im = psi_re * back_im - psi_im * back_re
        layer_grads.append(jnp.stack([grad_re, grad_im], axis=1))
        q_re = t_re * back_re + t_im * back_im
        q_im = t_re * back_im - t_im * back_re
        if layer > 0:
            back_re, back_im = propagate(q_re, q_im, tables, True)
    patch_grads = jnp.stack(layer_grads[::-1], axis=1)
    probe_term = jnp.stack([lax.optimization_barrier(jnp.sum(q_re, axis=0)), lax.optimization_barrier(jnp.sum(q_im, axis=0))], axis=0)
    return (patch_grads, probe_term)

def reference(object_slices, probe_field, scan_offsets, scan_count, measured):
    layers = object_slices.shape[0]
    window = probe_field.shape[1]

    def visit_tile(state_pair, tile_index):
        gradient, probe_sum = state_pair
        tile_row = tile_index // N_COL
        tile_col = tile_index % N_COL
        starts = scan_offsets[tile_row, tile_col]
        live_mask = (jnp.arange(SLOTS, dtype=jnp.int32) < scan_count[tile_row, tile_col]).astype(jnp.float32)

        def take_patch(start_row, start_col):
            anchor = (jnp.int32(0), jnp.int32(0), start_row.astype(jnp.int32), start_col.astype(jnp.int32))
            return lax.dynamic_slice(object_slices, anchor, (layers, 2, window, window))
        patches = jax.vmap(take_patch)(starts[0], starts[1])
        patch_grads, probe_term = slot_gradients(patches, probe_field, measured[tile_row, tile_col], live_mask)

        def place_slot(slot_index, accumulated):
            anchor = (jnp.int32(0), jnp.int32(0), starts[0, slot_index].astype(jnp.int32), starts[1, slot_index].astype(jnp.int32))
            current = lax.dynamic_slice(accumulated, anchor, (layers, 2, window, window))
            return lax.dynamic_update_slice(accumulated, current + patch_grads[slot_index], anchor)
        gradient = lax.fori_loop(0, SLOTS, place_slot, gradient)
        return ((gradient, probe_sum + probe_term), None)
    start_state = (jnp.zeros_like(object_slices), jnp.zeros((2, window, window), dtype=object_slices.dtype))
    final_state, unused = lax.scan(visit_tile, start_state, jnp.arange(N_ROW * N_COL, dtype=jnp.int32))
    gradient, probe_sum = final_state
    return (gradient, probe_sum / math.sqrt(POSITIONS))
```

```python
import functools
import math

import jax
import jax.numpy as jnp
import ml_dtypes
import numpy as np
from jax import lax
from jax.experimental import pallas as pl
from jax.experimental.pallas import tpu as pltpu
from jax.sharding import PartitionSpec as P

DEFOCUS = 0.3
FLOOR = 0.5


def real_form(m):
    return np.block([[m.real, -m.imag], [m.imag, m.real]])


def stage_matrices(window):
    half = window // 2
    index = np.arange(window)
    dft = np.exp(-2j * np.pi * (index[:, None] * index[None, :] % window) / window) / math.sqrt(window)
    freq = (index + half) % window - half
    phase = np.exp(-1j * np.pi * DEFOCUS * freq**2 / window)
    spread = dft.conj() @ (phase[:, None] * dft)
    near, far = spread[:half, :half], spread[:half, half:]
    parts = []
    for m in ((near + far) / 2, (near - far) / 2, dft[0::2, :half], dft[1::2, :half]):
        form = real_form(m)
        parts += [form, form.T]
    stack = []
    for form in parts:
        form = form.astype(np.float32)
        high = form.astype(ml_dtypes.bfloat16)
        low = (form - high.astype(np.float32)).astype(ml_dtypes.bfloat16)
        stack.append(np.concatenate([high, low], axis=1))
    return np.stack(stack)


PU, PU_T, PV, PV_T, FE, FE_T, FO, FO_T = range(8)


def split(x):
    high = x.astype(jnp.bfloat16)
    low = (x - high.astype(jnp.float32)).astype(jnp.bfloat16)
    return high, low


def dot(a, b):
    return jnp.dot(a, b, preferred_element_type=jnp.float32)


def from_left(w_ref, which, x):
    n = x.shape[0]
    high, low = split(x)
    wh, wl = w_ref[which, :, :n], w_ref[which, :, n:]
    return dot(wh, high) + dot(wh, low) + dot(wl, high)


def from_right(w_ref, which, x):
    n = x.shape[1]
    high, low = split(x)
    wh, wl = w_ref[which, :, :n], w_ref[which, :, n:]
    return dot(high, wh) + dot(low, wh) + dot(high, wl)


def rows(*parts):
    return jnp.concatenate(parts, axis=0)


def lanes(*parts):
    return jnp.concatenate(parts, axis=1)


def spread_field(w_ref, mats, xr, xi):
    u, v, ut, vt = mats
    h = xr.shape[0] // 2
    a = from_left(w_ref, u, rows(xr[:h] + xr[h:], xi[:h] + xi[h:]))
    b = from_left(w_ref, v, rows(xr[:h] - xr[h:], xi[:h] - xi[h:]))
    p, m = a + b, a - b
    yr, yi = rows(p[:h], m[:h]), rows(p[h:], m[h:])
    a = from_right(w_ref, ut, lanes(yr[:, :h] + yr[:, h:], yi[:, :h] + yi[:, h:]))
    b = from_right(w_ref, vt, lanes(yr[:, :h] - yr[:, h:], yi[:, :h] - yi[:, h:]))
    p, m = a + b, a - b
    return lanes(p[:, :h], m[:, :h]), lanes(p[:, h:], m[:, h:])


def to_far(w_ref, xr, xi):
    h = xr.shape[0] // 2
    e = from_left(w_ref, FE, rows(xr[:h] + xr[h:], xi[:h] + xi[h:]))
    o = from_left(w_ref, FO, rows(xr[:h] - xr[h:], xi[:h] - xi[h:]))
    yr, yi = rows(e[:h], o[:h]), rows(e[h:], o[h:])
    qe = from_right(w_ref, FE_T, lanes(yr[:, :h] + yr[:, h:], yi[:, :h] + yi[:, h:]))
    qo = from_right(w_ref, FO_T, lanes(yr[:, :h] - yr[:, h:], yi[:, :h] - yi[:, h:]))
    return qe, qo


def from_far(w_ref, ge, go):
    h = ge.shape[0] // 2
    a = from_right(w_ref, FE, ge)
    b = from_right(w_ref, FO, go)
    p, m = a + b, a - b
    yr, yi = lanes(p[:, :h], m[:, :h]), lanes(p[:, h:], m[:, h:])
    a = from_left(w_ref, FE_T, rows(yr[:h], yi[:h]))
    b = from_left(w_ref, FO_T, rows(yr[h:], yi[h:]))
    p, m = a + b, a - b
    return rows(p[:h], m[:h]), rows(p[h:], m[h:])


def window_kernel(rs_ref, cs_ref, count_ref, ext_ref, probe_ref, meas_ref, w_ref,
                  gext_ref, pg_ref, t_ref, psi_ref, m_ref):
    slots, n = meas_ref.shape[0], meas_ref.shape[1]
    h = n // 2
    gext_ref[...] = jnp.zeros_like(gext_ref)
    pg_ref[...] = jnp.zeros_like(pg_ref)
    lane = lax.broadcasted_iota(jnp.int32, (n + 8, h), 1)
    sub = lax.broadcasted_iota(jnp.int32, (n // 8, 8, h), 1)
    wide = lax.broadcasted_iota(jnp.int32, (n // 8 + 1, 8, h), 1)
    pick = lax.rem(lane[:n], h // 2) * 2
    first = lane[:n] < h // 2

    @pl.loop(0, slots)
    def _(s):
        r = rs_ref[s]
        c = cs_ref[s]
        base = lax.div(c, h)
        shift = c - base * h
        back = lax.rem(h - shift, h)
        top = pl.multiple_of(lax.div(r, 8) * 8, 8)
        down = r - top
        up = lax.rem(8 - down, 8)
        tall = n + 8
        for layer in range(2):
            for part in range(2):
                raw = [ext_ref[base + k, layer, part, pl.ds(top, tall), :] for k in range(3)]
                raw = [pltpu.roll(x, back, 1) for x in raw]
                for k in range(2):
                    x = jnp.where(lane < h - shift, raw[k], raw[k + 1])
                    x = pltpu.roll(x.reshape(tall // 8, 8, h), up, 1)
                    x = jnp.where(sub < 8 - down, x[:-1], x[1:])
                    t_ref[layer, part, :, k * h : (k + 1) * h] = x.reshape(n, h)
        pr, pi = probe_ref[0], probe_ref[1]
        tr, ti = t_ref[0, 0], t_ref[0, 1]
        xr, xi = spread_field(w_ref, (PU, PV, PU_T, PV_T), tr * pr - ti * pi, tr * pi + ti * pr)
        psi_ref[0] = xr
        psi_ref[1] = xi
        tr, ti = t_ref[1, 0], t_ref[1, 1]
        qe, qo = to_far(w_ref, tr * xr - ti * xi, tr * xi + ti * xr)
        live = jnp.where(s < count_ref[0], 1.0, 0.0).astype(jnp.float32)

        for par in range(2):
            got = [jnp.take_along_axis(meas_ref[s, :, k * h : (k + 1) * h], pick + par, axis=1) for k in range(2)]
            m_ref[par] = jnp.where(first, got[0], got[1])

        g = []
        for par, q in ((0, qe), (1, qo)):
            fr, fi = q[:, :h], q[:, h:]
            inv = lax.rsqrt(jnp.maximum(fr * fr + fi * fi, FLOOR * FLOOR))
            weight = live * (1.0 - rows(*[m_ref[par, pl.ds(rp, h, stride=2), :] for rp in range(2)]) * inv)
            g.append(lanes(weight * fr, weight * fi))
        br, bi = from_far(w_ref, *g)

        def place(layer, gr, gi):
            for part, x in ((0, gr), (1, gi)):
                moved = []
                for k in range(2):
                    y = pltpu.roll(x[:, k * h : (k + 1) * h].reshape(n // 8, 8, h), down, 1)
                    zero = jnp.zeros((1, 8, h), jnp.float32)
                    y = jnp.where(wide < down, rows(zero, y), rows(y, zero))
                    moved.append(pltpu.roll(y.reshape(tall, h), shift, 1))
                a, b = moved
                low = lane < shift
                zero = jnp.zeros_like(a)
                pieces = (jnp.where(low, zero, a), jnp.where(low, a, b), jnp.where(low, b, zero))
                for k, piece in enumerate(pieces):
                    where = (base + k, layer, part, pl.ds(top, tall), slice(None))
                    gext_ref[where] = gext_ref[where] + piece

        xr, xi = psi_ref[0], psi_ref[1]
        place(1, xr * br + xi * bi, xr * bi - xi * br)
        tr, ti = t_ref[1, 0], t_ref[1, 1]
        br, bi = spread_field(w_ref, (PU_T, PV_T, PU, PV), tr * br + ti * bi, tr * bi - ti * br)
        pr, pi = probe_ref[0], probe_ref[1]
        place(0, pr * br + pi * bi, pr * bi - pi * br)
        tr, ti = t_ref[0, 0], t_ref[0, 1]
        for part, x in ((0, tr * br + ti * bi), (1, tr * bi - ti * br)):
            for k in range(2):
                pg_ref[part * 2 + k] += x[:, k * h : (k + 1) * h]


def windows(rs, cs, count, ext, probe, meas, w):
    vmem = pl.BlockSpec(memory_space=pltpu.VMEM)
    smem = pl.BlockSpec(memory_space=pltpu.SMEM)
    n = probe.shape[1]
    return pl.pallas_call(
        window_kernel,
        out_shape=(jax.ShapeDtypeStruct(ext.shape, jnp.float32), jax.ShapeDtypeStruct((4, n, n // 2), jnp.float32)),
        in_specs=[smem, smem, smem, vmem, vmem, vmem, vmem],
        out_specs=(vmem, vmem),
        scratch_shapes=[pltpu.VMEM((2, 2, n, n), jnp.float32), pltpu.VMEM((2, n, n), jnp.float32),
                        pltpu.VMEM((2, n, n // 2), jnp.float32)],
        compiler_params=pltpu.CompilerParams(vmem_limit_bytes=48 << 20),
        name="windows",
    )(rs, cs, count, ext, probe, meas, w)


MESH = pl.DeviceIdType.MESH


def remote(src, dst, send, recv, target):
    return pltpu.make_async_remote_copy(
        src_ref=src, dst_ref=dst, send_sem=send, recv_sem=recv, device_id=target, device_id_type=MESH
    )


def greet(peers):
    barrier = pltpu.get_barrier_semaphore()
    total = 0
    for there, target in peers:
        @pl.when(there)
        def _(target=target):
            pl.semaphore_signal(barrier, inc=1, device_id=target, device_id_type=MESH)
        total = total + jnp.where(there, 1, 0)
    pl.semaphore_wait(barrier, total)


def neighbours():
    row, col = lax.axis_index("row"), lax.axis_index("col")
    n_row, n_col = lax.axis_size("row"), lax.axis_size("col")
    return {
        "up": (row > 0, {"row": row - 1, "col": col}),
        "down": (row < n_row - 1, {"row": row + 1, "col": col}),
        "left": (col > 0, {"row": row, "col": col - 1}),
        "right": (col < n_col - 1, {"row": row, "col": col + 1}),
    }


OPPOSITE = {"up": "down", "down": "up", "left": "right", "right": "left"}
SIDES = ("up", "down", "left", "right")


def halo_kernel(obj_ref, ext_ref, local_sem, send_sem, recv_sem):
    rows_, h = obj_ref.shape[2], ext_ref.shape[4]
    near = neighbours()
    top = slice(0, h), slice(0, h)
    greet([near[side] for side in SIDES])
    own = [pltpu.make_async_copy(obj_ref.at[:, :, :, pl.ds(b * h, h)], ext_ref.at[1 + b, :, :, pl.ds(h, rows_), :], local_sem.at[b]) for b in range(2)]
    first = []
    for layer in range(2):
        first.append((0 + layer, "right", obj_ref.at[layer, :, :, pl.ds(h, h)], ext_ref.at[0, layer, :, pl.ds(h, rows_), :]))
        first.append((2 + layer, "left", obj_ref.at[layer, :, :, pl.ds(0, h)], ext_ref.at[3, layer, :, pl.ds(h, rows_), :]))
        for b in range(2):
            first.append((4 + layer * 2 + b, "down", obj_ref.at[layer, :, pl.ds(rows_ - h, h), pl.ds(b * h, h)], ext_ref.at[1 + b, layer, :, pl.ds(0, h), :]))
            first.append((8 + layer * 2 + b, "up", obj_ref.at[layer, :, pl.ds(0, h), pl.ds(b * h, h)], ext_ref.at[1 + b, layer, :, pl.ds(rows_ + h, h), :]))
    copies = {}
    for number, side, src, dst in first:
        copies[number] = (side, remote(src, dst, send_sem.at[number], recv_sem.at[number], near[side][1]))
    for number in sorted(copies, key=lambda i: (i % 2 if i < 4 else (i - 4) // 2 % 2, i)):
        side, copy = copies[number]
        pl.when(near[side][0])(copy.start)
    for copy in own:
        copy.start()
    for layer in range(2):
        for b in range(2):
            side = ("left", "right")[b]
            for k, (source_side, start) in enumerate((("up", 0), ("down", rows_ + h))):
                came = (4, 8)[k] + layer * 2 + b
                number = 12 + layer * 4 + b * 2 + k
                block = ext_ref.at[1 + b, layer, :, pl.ds(start, h), :]
                copy = remote(block, ext_ref.at[(3, 0)[b], layer, :, pl.ds(start, h), :], send_sem.at[number], recv_sem.at[number], near[side][1])
                copies[number] = (side, copy)

                @pl.when(near[source_side][0])
                def _(came=came, side=side, copy=copy):
                    copies[came][1].wait_recv()
                    pl.when(near[side][0])(copy.start)
    for number, (side, copy) in copies.items():
        vertical = 4 <= number < 12
        corner = number >= 12
        source_side = ("up", "down")[number % 2] if corner else None

        def finish(copy=copy, side=side, vertical=vertical):
            pl.when(near[side][0])(copy.wait_send)
            if not vertical:
                pl.when(near[OPPOSITE[side]][0])(copy.wait_recv)

        if corner:
            pl.when(near[source_side][0])(finish)
        else:
            finish()
    for copy in own:
        copy.wait()


def halo(obj):
    layers, parts, rows_, cols = obj.shape
    h = cols // 2
    return pl.pallas_call(
        halo_kernel,
        out_shape=jax.ShapeDtypeStruct((4, layers, parts, rows_ + 2 * h, h), jnp.float32),
        in_specs=[pl.BlockSpec(memory_space=pl.ANY)],
        out_specs=pl.BlockSpec(memory_space=pltpu.VMEM),
        scratch_shapes=[pltpu.SemaphoreType.DMA((2,)), pltpu.SemaphoreType.DMA((20,)), pltpu.SemaphoreType.DMA((20,))],
        compiler_params=pltpu.CompilerParams(collective_id=0, has_side_effects=True, vmem_limit_bytes=16 << 20),
        name="halo",
    )(obj)


def back_kernel(gext_ref, pg_ref, side_ref, strip_ref, probe_ref,
                corner_ref, out_strip_ref, twin_ref, ring_ref, ring_sum_ref, group_ref, group_sum_ref,
                send_sem, recv_sem, group_send, group_recv, gather_send, gather_recv):
    h = gext_ref.shape[4]
    rows_ = gext_ref.shape[3] - 2 * h
    near = neighbours()
    row, col = lax.axis_index("row"), lax.axis_index("col")
    y, x_hi = lax.rem(row, 4), lax.div(row, 4)
    core, z, x_lo = lax.rem(col, 2), lax.rem(lax.div(col, 2), 8), lax.div(col, 16)
    group = x_hi * 16 + x_lo * 8 + z
    twin = {"row": row, "col": col + 1 - 2 * core}

    def ring_peer(k):
        return {"row": x_hi * 4 + lax.rem(y + k, 4), "col": col}

    def group_peer(k):
        g = lax.rem(group + k, 32)
        return {"row": lax.div(g, 16) * 4 + y, "col": lax.rem(g, 16) * 2 + core}, lax.rem(g, 16)

    def gather_peer(k):
        g = lax.rem(lax.rem(group, 16) + k, 16)
        return {"row": row, "col": g * 2 + core}

    barrier = pltpu.get_barrier_semaphore()
    total = 1 + 3 + 31
    for side in SIDES:
        there, target = near[side]

        @pl.when(there)
        def _(target=target):
            pl.semaphore_signal(barrier, inc=1, device_id=target, device_id_type=MESH)
        total = total + jnp.where(there, 1, 0)
    pl.semaphore_signal(barrier, inc=1, device_id=twin, device_id_type=MESH)
    for k in range(1, 4):
        pl.semaphore_signal(barrier, inc=1, device_id=ring_peer(k), device_id_type=MESH)

    @pl.loop(1, 32)
    def _(k):
        pl.semaphore_signal(barrier, inc=1, device_id=group_peer(k)[0], device_id_type=MESH)
    pl.semaphore_wait(barrier, total)

    def copy(number, src, dst, target):
        return remote(src, dst, send_sem.at[number], recv_sem.at[number], target)

    def at(start):
        return pl.ds(start, h)

    lows = (0, rows_ + h)
    corners = {}
    for b, side in enumerate(("left", "right")):
        for k in range(2):
            corners[b, k] = copy(b * 2 + k, gext_ref.at[b * 3, :, :, at(lows[k]), :], corner_ref.at[b, k], near[side][1])
            pl.when(near[side][0])(corners[b, k].start)
    twin_copy = copy(10, pg_ref.at[1 - core], twin_ref, twin)
    twin_copy.start()
    sides = {}
    for b, side in enumerate(("left", "right")):
        sides[b] = copy(4 + b, gext_ref.at[b * 3, :, :, pl.ds(h, rows_), :], side_ref.at[b], near[side][1])
        pl.when(near[side][0])(sides[b].start)

    strips = {}
    for k, side in enumerate(("up", "down")):
        for b in range(2):
            out_strip_ref[k, b] = gext_ref[1 + b, :, :, at(lows[k]), :]
            source = ("left", "right")[b]

            @pl.when(near[source][0])
            def _(k=k, b=b):
                corners[1 - b, k].wait_recv()
                out_strip_ref[k, b] += corner_ref[1 - b, k]
            strips[k, b] = copy(6 + k * 2 + b, out_strip_ref.at[k, b], strip_ref.at[k, b], near[side][1])
            pl.when(near[side][0])(strips[k, b].start)

    twin_copy.wait_recv()
    ring_ref[0] = pg_ref[core] + twin_ref[...]
    rings = []
    for k in range(1, 4):
        rings.append(copy(10 + k, ring_ref.at[0, lax.rem(y + k, 4)], ring_ref.at[k, 0], ring_peer(k)))
        rings[-1].start()
    for r in rings:
        r.wait_recv()
    ring_sum_ref[...] = ring_ref[0, y] + ring_ref[1, 0] + ring_ref[2, 0] + ring_ref[3, 0]

    def group_copy(k):
        target, piece = group_peer(k)
        return remote(ring_sum_ref.at[piece], group_ref.at[k], group_send.at[k], group_recv.at[k], target)

    @pl.loop(1, 32)
    def _(k):
        group_copy(k).start()
    mine = lax.rem(group, 16)
    group_ref[0] = ring_sum_ref[mine]

    @pl.loop(1, 32)
    def _(k):
        group_copy(k).wait_recv()
    group_sum_ref[mine] = jnp.sum(group_ref[...], axis=0)

    def gather_copy(k):
        return remote(group_sum_ref.at[mine], group_sum_ref.at[mine], gather_send.at[k], gather_recv.at[k], gather_peer(k))

    @pl.loop(1, 16)
    def _(k):
        gather_copy(k).start()

    @pl.loop(1, 16)
    def _(k):
        gather_copy(k).wait_recv()
    probe_ref[core, y] = group_sum_ref[...]
    gathers = []
    for k in range(1, 4):
        gathers.append(copy(13 + k, group_sum_ref, probe_ref.at[core, y], ring_peer(k)))
        gathers[-1].start()
    for g in gathers:
        g.wait_recv()
    last = copy(17, probe_ref.at[core], probe_ref.at[core], twin)
    last.start()
    last.wait_recv()

    for b, side in enumerate(("left", "right")):
        for k in range(2):
            pl.when(near[side][0])(corners[b, k].wait_send)
        pl.when(near[side][0])(sides[b].wait_send)
        pl.when(near[OPPOSITE[side]][0])(sides[b].wait_recv)
    for k, side in enumerate(("up", "down")):
        for b in range(2):
            pl.when(near[side][0])(strips[k, b].wait_send)
            pl.when(near[OPPOSITE[side]][0])(strips[k, b].wait_recv)
    twin_copy.wait_send()
    for c in rings + gathers + [last]:
        c.wait_send()

    @pl.loop(1, 32)
    def _(k):
        group_copy(k).wait_send()

    @pl.loop(1, 16)
    def _(k):
        gather_copy(k).wait_send()


def back(gext, pg):
    _, layers, parts, tall, h = gext.shape
    rows_ = tall - 2 * h
    vmem = pl.BlockSpec(memory_space=pltpu.VMEM)
    f32 = jnp.float32
    return pl.pallas_call(
        back_kernel,
        out_shape=(
            jax.ShapeDtypeStruct((2, layers, parts, rows_, h), f32),
            jax.ShapeDtypeStruct((2, 2, layers, parts, h, h), f32),
            jax.ShapeDtypeStruct((2, 4, 16, 8, 128), f32),
        ),
        in_specs=[vmem, vmem],
        out_specs=(vmem, vmem, vmem),
        scratch_shapes=[
            pltpu.VMEM((2, 2, layers, parts, h, h), f32),
            pltpu.VMEM((2, 2, layers, parts, h, h), f32),
            pltpu.VMEM((4, 16, 8, 128), f32),
            pltpu.VMEM((4, 4, 16, 8, 128), f32),
            pltpu.VMEM((16, 8, 128), f32),
            pltpu.VMEM((32, 8, 128), f32),
            pltpu.VMEM((16, 8, 128), f32),
            pltpu.SemaphoreType.DMA((18,)),
            pltpu.SemaphoreType.DMA((18,)),
            pltpu.SemaphoreType.DMA((32,)),
            pltpu.SemaphoreType.DMA((32,)),
            pltpu.SemaphoreType.DMA((16,)),
            pltpu.SemaphoreType.DMA((16,)),
        ],
        compiler_params=pltpu.CompilerParams(collective_id=1, has_side_effects=True, vmem_limit_bytes=32 << 20),
        name="back",
    )(gext, pg)


def join_kernel(n_row, n_col, place_ref, gext_ref, side_ref, strip_ref, out_ref):
    row, col = place_ref[0], place_ref[1]
    h = gext_ref.shape[4]
    rows_ = gext_ref.shape[3] - 2 * h
    for b in range(2):
        where = pl.ds(b * h, h)
        out_ref[:, :, :, where] = gext_ref[1 + b, :, :, pl.ds(h, rows_), :]

        @pl.when(col < n_col - 1 if b == 1 else col > 0)
        def _():
            out_ref[:, :, :, where] += side_ref[1 - b]

        @pl.when(row < n_row - 1)
        def _():
            out_ref[:, :, pl.ds(rows_ - h, h), where] += strip_ref[0, b]

        @pl.when(row > 0)
        def _():
            out_ref[:, :, pl.ds(0, h), where] += strip_ref[1, b]


def join(place, gext, side, strip):
    _, layers, parts, tall, h = gext.shape
    vmem = pl.BlockSpec(memory_space=pltpu.VMEM)
    return pl.pallas_call(
        functools.partial(join_kernel, lax.axis_size("row"), lax.axis_size("col")),
        out_shape=jax.ShapeDtypeStruct((layers, parts, tall - 2 * h, 2 * h), jnp.float32),
        in_specs=[pl.BlockSpec(memory_space=pltpu.SMEM), vmem, vmem, vmem],
        out_specs=vmem,
        compiler_params=pltpu.CompilerParams(vmem_limit_bytes=32 << 20),
        name="join",
    )(place, gext, side, strip)


def local(w, object_slices, probe_field, scan_offsets, scan_count, measured):
    layers, parts, tile_rows, tile_cols = object_slices.shape
    n = probe_field.shape[1]
    row, col = lax.axis_index("row"), lax.axis_index("col")
    ext = halo(object_slices)
    rs = scan_offsets[0, 0, 0] - row * tile_rows + n // 2
    cs = scan_offsets[0, 0, 1] - col * tile_cols + n // 2
    gext, pg = windows(rs, cs, scan_count[0], ext, probe_field, measured[0, 0], w)
    side, strip, total = back(gext, pg.reshape(2, 4, 16, 8, 128))
    object_grad = join(jnp.stack([row, col]).astype(jnp.int32), gext, side, strip)
    positions = lax.axis_size("row") * lax.axis_size("col") * measured.shape[2]
    probe_grad = total.reshape(2, 2, n, n // 2).transpose(0, 2, 1, 3).reshape(2, n, n) / math.sqrt(positions)
    return object_grad, probe_grad


def solution(mesh):
    placed = (
        P(None, None, "row", "col"),
        P(),
        P("row", "col", None, None),
        P("row", "col"),
        P("row", "col", None, None, None),
    )
    w = stage_matrices(256)
    return jax.shard_map(
        lambda *args: local(jnp.asarray(w), *args),
        mesh=mesh,
        in_specs=placed,
        out_specs=(P(None, None, "row", "col"), P()),
        check_vma=False,
    )
```

```python
import functools
import math

import jax
import jax.numpy as jnp
import ml_dtypes
import numpy as np
from jax import lax
from jax.experimental import pallas as pl
from jax.experimental.pallas import tpu as pltpu
from jax.sharding import PartitionSpec as P

DEFOCUS = 0.3
FLOOR = 0.5


def real_form(m):
    return np.block([[m.real, -m.imag], [m.imag, m.real]])


def stage_matrices(window):
    half = window // 2
    index = np.arange(window)
    dft = np.exp(-2j * np.pi * (index[:, None] * index[None, :] % window) / window) / math.sqrt(window)
    freq = (index + half) % window - half
    phase = np.exp(-1j * np.pi * DEFOCUS * freq**2 / window)
    spread = dft.conj() @ (phase[:, None] * dft)
    near, far = spread[:half, :half], spread[:half, half:]
    stack = []
    for m in ((near + far) / 2, (near - far) / 2, dft[0::2, :half], dft[1::2, :half]):
        for form in (real_form(m), real_form(m).T):
            form = form.astype(np.float32)
            high = form.astype(ml_dtypes.bfloat16)
            low = (form - high.astype(np.float32)).astype(ml_dtypes.bfloat16)
            stack.append(np.concatenate([high, low], axis=1))
    return np.stack(stack)


PU, PU_T, PV, PV_T, FE, FE_T, FO, FO_T = range(8)


def split(x):
    high = x.astype(jnp.bfloat16)
    low = (x - high.astype(jnp.float32)).astype(jnp.bfloat16)
    return high, low


def dot(a, b):
    return jnp.dot(a, b, preferred_element_type=jnp.float32)


def from_left(w_ref, which, x):
    n = x.shape[0]
    high, low = split(x)
    wh, wl = w_ref[which, :, :n], w_ref[which, :, n:]
    return dot(wh, high) + dot(wh, low) + dot(wl, high)


def from_right(w_ref, which, x):
    n = x.shape[1]
    high, low = split(x)
    wh, wl = w_ref[which, :, :n], w_ref[which, :, n:]
    return dot(high, wh) + dot(low, wh) + dot(high, wl)


def rows(*parts):
    return jnp.concatenate(parts, axis=0)


def lanes(*parts):
    return jnp.concatenate(parts, axis=1)


def spread_field(w_ref, mats, xr, xi):
    u, v, ut, vt = mats
    h = xr.shape[0] // 2
    a = from_left(w_ref, u, rows(xr[:h] + xr[h:], xi[:h] + xi[h:]))
    b = from_left(w_ref, v, rows(xr[:h] - xr[h:], xi[:h] - xi[h:]))
    p, m = a + b, a - b
    yr, yi = rows(p[:h], m[:h]), rows(p[h:], m[h:])
    a = from_right(w_ref, ut, lanes(yr[:, :h] + yr[:, h:], yi[:, :h] + yi[:, h:]))
    b = from_right(w_ref, vt, lanes(yr[:, :h] - yr[:, h:], yi[:, :h] - yi[:, h:]))
    p, m = a + b, a - b
    return lanes(p[:, :h], m[:, :h]), lanes(p[:, h:], m[:, h:])


def to_far(w_ref, xr, xi):
    h = xr.shape[0] // 2
    e = from_left(w_ref, FE, rows(xr[:h] + xr[h:], xi[:h] + xi[h:]))
    o = from_left(w_ref, FO, rows(xr[:h] - xr[h:], xi[:h] - xi[h:]))
    yr, yi = rows(e[:h], o[:h]), rows(e[h:], o[h:])
    qe = from_right(w_ref, FE_T, lanes(yr[:, :h] + yr[:, h:], yi[:, :h] + yi[:, h:]))
    qo = from_right(w_ref, FO_T, lanes(yr[:, :h] - yr[:, h:], yi[:, :h] - yi[:, h:]))
    return qe, qo


def from_far(w_ref, ge, go):
    h = ge.shape[0] // 2
    a = from_right(w_ref, FE, ge)
    b = from_right(w_ref, FO, go)
    p, m = a + b, a - b
    yr, yi = lanes(p[:, :h], m[:, :h]), lanes(p[:, h:], m[:, h:])
    a = from_left(w_ref, FE_T, rows(yr[:h], yi[:h]))
    b = from_left(w_ref, FO_T, rows(yr[h:], yi[h:]))
    p, m = a + b, a - b
    return rows(p[:h], m[:h]), rows(p[h:], m[h:])


def one_hot(n, shift, across):
    a = lax.broadcasted_iota(jnp.int32, (n, n), 0)
    b = lax.broadcasted_iota(jnp.int32, (n, n), 1)
    gap = b - a - shift if across else a - b - shift
    return jnp.where((gap == 0) | (gap == -n), 1.0, 0.0).astype(jnp.bfloat16)


def take_left(m, x):
    high, low = split(x)
    return dot(m, high) + dot(m, low)


def take_right(x, m):
    high, low = split(x)
    return dot(high, m) + dot(low, m)


def move_probe(rs_ref, cs_ref, probe_ref, p_ref):
    n = probe_ref.shape[1]

    def one(s, carry):
        x = take_left(one_hot(n, lax.rem(rs_ref[s], n), False), lanes(probe_ref[0], probe_ref[1]))
        x = take_right(rows(x[:, :n], x[:, n:]), one_hot(n, lax.rem(cs_ref[s], n), True))
        p_ref[s, 0], p_ref[s, 1] = x[:n], x[n:]
        return carry

    lax.fori_loop(0, p_ref.shape[0], one, 0)


def far_order(meas_ref, m_ref):
    slots, n = meas_ref.shape[0], meas_ref.shape[1]
    h = n // 2
    lane = lax.broadcasted_iota(jnp.int32, (n, h), 1)
    pick = lax.rem(lane, h // 2) * 2

    def one(s, carry):
        for par in range(2):
            got = [jnp.take_along_axis(meas_ref[s, :, k * h : (k + 1) * h], pick + par, axis=1) for k in range(2)]
            m_ref[s, par] = jnp.where(lane < h // 2, got[0], got[1])
        return carry

    lax.fori_loop(0, slots, one, 0)


def cut_windows(layer, rs_ref, cs_ref, ext_ref, t_ref):
    slots, n = t_ref.shape[1], t_ref.shape[3]
    h = n // 2
    step = n // 4

    def one(i, carry):
        at = pl.multiple_of(i * step, step)
        row = lax.broadcasted_iota(jnp.int32, (step, h), 0) + at
        lane = lax.broadcasted_iota(jnp.int32, (step, h), 1)
        for part in range(2):
            for k in range(2):
                blocks = [[ext_ref[layer, 2 * w + k, part, pl.ds(m * n + at, step), :] for m in range(3)] for w in range(2)]
                for s in range(slots):
                    r, c = rs_ref[s], cs_ref[s]
                    halves = [jnp.where(row >= r, e[0], jnp.where(row >= r - n, e[1], e[2])) for e in blocks]
                    t_ref[layer, s, part, pl.ds(at, step), k * h : (k + 1) * h] = jnp.where(lane + k * h >= c, halves[0], halves[1])
        return carry

    lax.fori_loop(0, n // step, one, 0)


def forward(w_ref, p_ref, t_ref, psi_ref):
    def one(s, carry):
        pr, pi = p_ref[s, 0], p_ref[s, 1]
        tr, ti = t_ref[0, s, 0], t_ref[0, s, 1]
        psi_ref[s, 0], psi_ref[s, 1] = spread_field(w_ref, (PU, PV, PU_T, PV_T), tr * pr - ti * pi, tr * pi + ti * pr)
        return carry

    lax.fori_loop(0, t_ref.shape[1], one, 0, unroll=True)


def far_and_back(w_ref, count_ref, m_ref, t_ref, psi_ref, q_ref, patch_ref):
    h = t_ref.shape[3] // 2

    def one(s, carry):
        xr, xi = psi_ref[s, 0], psi_ref[s, 1]
        tr, ti = t_ref[1, s, 0], t_ref[1, s, 1]
        far = to_far(w_ref, tr * xr - ti * xi, tr * xi + ti * xr)
        live = jnp.where(s < count_ref[0], 1.0, 0.0).astype(jnp.float32)
        g = []
        for par, f in enumerate(far):
            fr, fi = f[:, :h], f[:, h:]
            inv = lax.rsqrt(jnp.maximum(fr * fr + fi * fi, FLOOR * FLOOR))
            amps = rows(*[m_ref[s, par, pl.ds(p, h, stride=2), :] for p in range(2)])
            weight = live * (1.0 - amps * inv)
            g.append(lanes(weight * fr, weight * fi))
        br, bi = from_far(w_ref, *g)
        xr, xi = psi_ref[s, 0], psi_ref[s, 1]
        patch_ref[s, 0] = xr * br + xi * bi
        patch_ref[s, 1] = xr * bi - xi * br
        tr, ti = t_ref[1, s, 0], t_ref[1, s, 1]
        q_ref[s, 0] = tr * br + ti * bi
        q_ref[s, 1] = tr * bi - ti * br
        return carry

    lax.fori_loop(0, t_ref.shape[1], one, 0, unroll=True)


def backward(w_ref, rs_ref, cs_ref, p_ref, t_ref, q_ref, patch_ref, pg_ref):
    n = t_ref.shape[3]
    h = n // 2
    pg_ref[...] = jnp.zeros_like(pg_ref)

    def one(s, carry):
        br, bi = spread_field(w_ref, (PU_T, PV_T, PU, PV), q_ref[s, 0], q_ref[s, 1])
        pr, pi = p_ref[s, 0], p_ref[s, 1]
        patch_ref[s, 0] = pr * br + pi * bi
        patch_ref[s, 1] = pr * bi - pi * br
        tr, ti = t_ref[0, s, 0], t_ref[0, s, 1]
        x = rows(tr * br + ti * bi, tr * bi - ti * br)
        x = take_right(x, one_hot(n, n - lax.rem(cs_ref[s], n), True))
        x = take_left(one_hot(n, n - lax.rem(rs_ref[s], n), False), lanes(x[:n], x[n:]))
        for part in range(2):
            for k in range(2):
                start = part * n + k * h
                spot = part, pl.ds(2 * k, 2)
                pg_ref[spot] += x[:, start : start + h].reshape((2,) + pg_ref.shape[2:])
        return carry

    lax.fori_loop(0, t_ref.shape[1], one, 0, unroll=True)


def add_patches(layer, rs_ref, cs_ref, patch_ref, gext_ref):
    slots, n = patch_ref.shape[0], patch_ref.shape[2]
    h = n // 2
    step = n // 8

    def one(i, carry):
        at = pl.multiple_of(i * step, step)
        row = lax.broadcasted_iota(jnp.int32, (step, h), 0) + at
        lane = lax.broadcasted_iota(jnp.int32, (step, h), 1)
        for part in range(2):
            for k in range(2):
                sums = [[None] * 3, [None] * 3]
                for s in range(slots):
                    r, c = rs_ref[s], cs_ref[s]
                    x = patch_ref[s, part, pl.ds(at, step), k * h : (k + 1) * h]
                    zero = jnp.zeros_like(x)
                    left = lane + k * h >= c
                    for w, y in enumerate((jnp.where(left, x, zero), jnp.where(left, zero, x))):
                        first, third = row >= r, row < r - n
                        parts = (jnp.where(first, y, zero), jnp.where(first | third, zero, y), jnp.where(third, y, zero))
                        for m in range(3):
                            sums[w][m] = parts[m] if sums[w][m] is None else sums[w][m] + parts[m]
                for w in range(2):
                    for m in range(3):
                        gext_ref[layer, 2 * w + k, part, pl.ds(m * n + at, step), :] = sums[w][m]
        return carry

    lax.fori_loop(0, n // step, one, 0)


MESH = pl.DeviceIdType.MESH
SIDES = ("up", "down", "left", "right")
OPPOSITE = {"up": "down", "down": "up", "left": "right", "right": "left"}


def step_kernel(rs_ref, cs_ref, count_ref, obj_hbm, probe_hbm, meas_hbm, w_hbm,
                grad_ref, total_ref,
                w_ref, probe_ref, meas_ref, ext_ref, gext_ref, t_ref, psi_ref, m_ref, q_ref, patch_ref, p_ref,
                corner_ref, side_ref, strip_ref, out_strip_ref,
                pg_ref, twin_ref, xs_ref, xr_ref, zs_ref, zr_ref, yr_ref, za_ref,
                local_sem, send_sem, recv_sem, sum_send, sum_recv):
    h = ext_ref.shape[4]
    tile = ext_ref.shape[3] - 2 * h
    row, col = lax.axis_index("row"), lax.axis_index("col")
    n_row, n_col = lax.axis_size("row"), lax.axis_size("col")
    near = {
        "up": (row > 0, {"row": row - 1, "col": col}),
        "down": (row < n_row - 1, {"row": row + 1, "col": col}),
        "left": (col > 0, {"row": row, "col": col - 1}),
        "right": (col < n_col - 1, {"row": row, "col": col + 1}),
    }
    y, x_hi = lax.rem(row, 4), lax.div(row, 4)
    core, z, x_lo = lax.rem(col, 2), lax.rem(lax.div(col, 2), 8), lax.div(col, 16)
    x = x_hi * 2 + x_lo
    twin = {"row": row, "col": col + 1 - 2 * core}

    def x_peer(k):
        other = lax.rem(x + k, 4)
        return {"row": lax.div(other, 2) * 4 + y, "col": lax.rem(other, 2) * 16 + z * 2 + core}

    def y_peer(k):
        return {"row": x_hi * 4 + lax.rem(y + k, 4), "col": col}

    def z_peer(k):
        return {"row": row, "col": x_lo * 16 + lax.rem(z + k, 8) * 2 + core}

    def send(number, src, dst, target, layer=None):
        sems = (sum_send.at[number], sum_recv.at[number]) if layer is None else (send_sem.at[layer, number], recv_sem.at[layer, number])
        return pltpu.make_async_remote_copy(src_ref=src, dst_ref=dst, send_sem=sems[0], recv_sem=sems[1], device_id=target, device_id_type=MESH)

    barrier = pltpu.get_barrier_semaphore()

    def greet(target):
        pl.semaphore_signal(barrier, inc=1, device_id=target, device_id_type=MESH)

    expected = 1 + 3 + 3 + 7
    for there, target in near.values():
        pl.when(there)(functools.partial(greet, target))
        expected = expected + jnp.where(there, 1, 0)
    for target in [twin] + [x_peer(k) for k in range(1, 4)] + [y_peer(k) for k in range(1, 4)] + [z_peer(k) for k in range(1, 8)]:
        greet(target)

    own = [pltpu.make_async_copy(meas_hbm, meas_ref, local_sem.at[0]),
           pltpu.make_async_copy(probe_hbm, probe_ref, local_sem.at[1]),
           pltpu.make_async_copy(w_hbm, w_ref, local_sem.at[2])]
    for layer in range(2):
        for b in range(2):
            own.append(pltpu.make_async_copy(obj_hbm.at[layer, :, :, pl.ds(b * h, h)], ext_ref.at[layer, 1 + b, :, pl.ds(h, tile), :], local_sem.at[3 + layer * 2 + b]))
    for c in own:
        c.start()
    own[0].wait()
    far_order(meas_ref, m_ref)
    own[1].wait()
    pl.semaphore_wait(barrier, expected)

    low = (0, tile + h)
    halo = [{}, {}]
    for layer in range(2):
        c = halo[layer]
        c[0] = "right", send(0, obj_hbm.at[layer, :, :, pl.ds(h, h)], ext_ref.at[layer, 0, :, pl.ds(h, tile), :], near["right"][1], layer)
        c[1] = "left", send(1, obj_hbm.at[layer, :, :, pl.ds(0, h)], ext_ref.at[layer, 3, :, pl.ds(h, tile), :], near["left"][1], layer)
        for b in range(2):
            c[2 + b] = "down", send(2 + b, obj_hbm.at[layer, :, pl.ds(tile - h, h), pl.ds(b * h, h)], ext_ref.at[layer, 1 + b, :, pl.ds(0, h), :], near["down"][1], layer)
            c[4 + b] = "up", send(4 + b, obj_hbm.at[layer, :, pl.ds(0, h), pl.ds(b * h, h)], ext_ref.at[layer, 1 + b, :, pl.ds(tile + h, h), :], near["up"][1], layer)
            for k in range(2):
                block = ext_ref.at[layer, 1 + b, :, pl.ds(low[k], h), :]
                side = ("left", "right")[b]
                c[6 + b * 2 + k] = side, send(6 + b * 2 + k, block, ext_ref.at[layer, (3, 0)[b], :, pl.ds(low[k], h), :], near[side][1], layer)

    def start(layer, numbers):
        for number in numbers:
            side, c = halo[layer][number]
            pl.when(near[side][0])(c.start)

    def forward_corners(layer):
        for b in range(2):
            for k in range(2):
                @pl.when(near[("up", "down")[k]][0])
                def _(b=b, k=k):
                    halo[layer][(2, 4)[k] + b][1].wait_recv()
                    start(layer, [6 + b * 2 + k])

    def halo_in(layer):
        own[3 + layer * 2].wait()
        own[4 + layer * 2].wait()
        for number in (0, 1, 6, 7, 8, 9):
            side, c = halo[layer][number]

            def arrive(side=side, c=c):
                pl.when(near[OPPOSITE[side]][0])(c.wait_recv)
            if number < 2:
                arrive()
            else:
                pl.when(near[("up", "down")[number % 2]][0])(arrive)

    start(0, (0, 1, 2, 3, 4, 5))
    start(1, (2, 3, 4, 5))
    forward_corners(0)
    start(1, (0, 1))
    move_probe(rs_ref, cs_ref, probe_ref, p_ref)
    own[2].wait()
    halo_in(0)
    cut_windows(0, rs_ref, cs_ref, ext_ref, t_ref)
    forward(w_ref, p_ref, t_ref, psi_ref)
    forward_corners(1)
    halo_in(1)
    cut_windows(1, rs_ref, cs_ref, ext_ref, t_ref)
    far_and_back(w_ref, count_ref, m_ref, t_ref, psi_ref, q_ref, patch_ref)
    add_patches(1, rs_ref, cs_ref, patch_ref, gext_ref)

    back = [{}, {}]
    for layer in range(2):
        for b, side in enumerate(("left", "right")):
            for k in range(2):
                number = 10 + b * 2 + k
                back[layer][number] = side, send(number, gext_ref.at[layer, b * 3, :, pl.ds(low[k], h), :], corner_ref.at[layer, b, k], near[side][1], layer)
            back[layer][14 + b] = side, send(14 + b, gext_ref.at[layer, b * 3, :, pl.ds(h, tile), :], side_ref.at[layer, b], near[side][1], layer)
        for k, side in enumerate(("up", "down")):
            for b in range(2):
                number = 16 + k * 2 + b
                back[layer][number] = side, send(number, out_strip_ref.at[layer, k, b], strip_ref.at[layer, k, b], near[side][1], layer)

    def start_back(layer, numbers):
        for number in numbers:
            side, c = back[layer][number]
            pl.when(near[side][0])(c.start)

    def strips_out(layer):
        for k in range(2):
            for b in range(2):
                out_strip_ref[layer, k, b] = gext_ref[layer, 1 + b, :, pl.ds(low[k], h), :]

                @pl.when(near[("left", "right")[b]][0])
                def _(k=k, b=b):
                    back[layer][10 + (1 - b) * 2 + k][1].wait_recv()
                    out_strip_ref[layer, k, b] += corner_ref[layer, 1 - b, k]
                start_back(layer, [16 + k * 2 + b])

    def join(layer):
        for b in range(2):
            where = pl.ds(b * h, h)
            grad_ref[layer, :, :, where] = gext_ref[layer, 1 + b, :, pl.ds(h, tile), :]

            @pl.when(near[("left", "right")[b]][0])
            def _(b=b, where=where):
                back[layer][14 + 1 - b][1].wait_recv()
                grad_ref[layer, :, :, where] += side_ref[layer, 1 - b]

            @pl.when(near["down"][0])
            def _(b=b, where=where):
                back[layer][16 + b][1].wait_recv()
                grad_ref[layer, :, pl.ds(tile - h, h), where] += strip_ref[layer, 0, b]

            @pl.when(near["up"][0])
            def _(b=b, where=where):
                back[layer][18 + b][1].wait_recv()
                grad_ref[layer, :, pl.ds(0, h), where] += strip_ref[layer, 1, b]

    start_back(1, range(10, 16))
    backward(w_ref, rs_ref, cs_ref, p_ref, t_ref, q_ref, patch_ref, pg_ref)

    sums = [send(0, pg_ref.at[1 - core], twin_ref, twin)]
    sums[0].start()
    add_patches(0, rs_ref, cs_ref, patch_ref, gext_ref)
    start_back(0, range(10, 14))
    sums[0].wait_recv()
    xs_ref[...] = pg_ref[core] + twin_ref[...]

    def exchange(copies):
        for c in copies:
            c.start()
        sums.extend(copies)
        return copies

    def arrive(copies):
        for c in copies:
            c.wait_recv()

    along_x = exchange([send(k, xs_ref.at[lax.rem(x + k, 4)], xr_ref.at[k - 1], x_peer(k)) for k in range(1, 4)])
    strips_out(1)
    arrive(along_x)
    zs_ref[...] = xs_ref[x] + xr_ref[0] + xr_ref[1] + xr_ref[2]
    along_z = exchange([send(3 + k, zs_ref.at[lax.rem(z + k, 8)], zr_ref.at[k - 1], z_peer(k)) for k in range(1, 8)])
    start_back(0, (14, 15))
    arrive(along_z)
    yr_ref[y] = zs_ref[z] + jnp.sum(zr_ref[...], axis=0)
    along_y = exchange([send(10 + k, yr_ref.at[y], yr_ref.at[y], y_peer(k)) for k in range(1, 4)])
    strips_out(0)
    arrive(along_y)
    za_ref[z] = yr_ref[0] + yr_ref[1] + yr_ref[2] + yr_ref[3]
    along_z = exchange([send(13 + k, za_ref.at[z], za_ref.at[z], z_peer(k)) for k in range(1, 8)])
    arrive(along_z)
    total_ref[core, x] = za_ref[...]
    along_x = exchange([send(20 + k, za_ref, total_ref.at[core, x], x_peer(k)) for k in range(1, 4)])
    join(1)
    arrive(along_x)
    last = exchange([send(24, total_ref.at[core], total_ref.at[core], twin)])
    join(0)
    arrive(last)

    for c in sums:
        c.wait_send()
    for layer in range(2):
        for number, (side, c) in list(halo[layer].items()) + list(back[layer].items()):
            def sent(side=side, c=c):
                pl.when(near[side][0])(c.wait_send)
            if 6 <= number < 10:
                pl.when(near[("up", "down")[number % 2]][0])(sent)
            else:
                sent()


def step(rs, cs, count, obj, probe, meas, w):
    layers, parts, tile, _ = obj.shape
    n = probe.shape[1]
    h = n // 2
    slots = meas.shape[0]
    smem, vmem, hbm = (pl.BlockSpec(memory_space=s) for s in (pltpu.SMEM, pltpu.VMEM, pltpu.HBM))
    f32 = jnp.float32
    shapes = [
        probe.shape, meas.shape,
        (layers, 4, parts, tile + n, h), (layers, 4, parts, tile + n, h),
        (layers, slots, parts, n, n), (slots, parts, n, n), (slots, 2, n, h), (slots, parts, n, n),
        (slots, parts, n, n), (slots, parts, n, n),
        (layers, 2, 2, parts, h, h), (layers, 2, parts, tile, h), (layers, 2, 2, parts, h, h), (layers, 2, 2, parts, h, h),
        (2, 4, 8, 16, 128), (4, 8, 16, 128), (4, 8, 16, 128), (3, 8, 16, 128), (8, 16, 128), (7, 16, 128), (4, 16, 128), (8, 16, 128),
    ]
    dma = pltpu.SemaphoreType.DMA
    return pl.pallas_call(
        step_kernel,
        out_shape=(jax.ShapeDtypeStruct(obj.shape, f32), jax.ShapeDtypeStruct((2, 4, 8, 16, 128), f32)),
        in_specs=[smem, smem, smem, hbm, hbm, hbm, hbm],
        out_specs=(vmem, vmem),
        scratch_shapes=[pltpu.VMEM(w.shape, w.dtype)] + [pltpu.VMEM(s, f32) for s in shapes]
        + [dma((7,)), dma((2, 20)), dma((2, 20)), dma((25,)), dma((25,))],
        compiler_params=pltpu.CompilerParams(collective_id=0, has_side_effects=True, vmem_limit_bytes=56 << 20),
        name="step",
    )(rs, cs, count, obj, probe, meas, w)


def local(w, object_slices, probe_field, scan_offsets, scan_count, measured):
    _, _, tile_rows, tile_cols = object_slices.shape
    n = probe_field.shape[1]
    rs = scan_offsets[0, 0, 0] - lax.axis_index("row") * tile_rows + n // 2
    cs = scan_offsets[0, 0, 1] - lax.axis_index("col") * tile_cols + n // 2
    object_grad, total = step(rs, cs, scan_count[0], object_slices, probe_field, measured[0, 0], w)
    positions = lax.axis_size("row") * lax.axis_size("col") * measured.shape[2]
    probe_grad = total.reshape(2, 2, n, n // 2).transpose(0, 2, 1, 3).reshape(2, n, n) / math.sqrt(positions)
    return object_grad, probe_grad


def solution(mesh):
    placed = (
        P(None, None, "row", "col"),
        P(),
        P("row", "col", None, None),
        P("row", "col"),
        P("row", "col", None, None, None),
    )
    w = stage_matrices(256)
    return jax.shard_map(
        lambda *args: local(jnp.asarray(w), *args),
        mesh=mesh,
        in_specs=placed,
        out_specs=(P(None, None, "row", "col"), P()),
        check_vma=False,
    )
```

```python
import functools
import math

import jax
import jax.numpy as jnp
import ml_dtypes
import numpy as np
from jax import lax
from jax.experimental import pallas as pl
from jax.experimental.pallas import tpu as pltpu
from jax.sharding import PartitionSpec as P

DEFOCUS = 0.3
FLOOR = 0.5


def real_form(m):
    return np.block([[m.real, -m.imag], [m.imag, m.real]])


def stage_matrices(window):
    half = window // 2
    index = np.arange(window)
    dft = np.exp(-2j * np.pi * (index[:, None] * index[None, :] % window) / window) / math.sqrt(window)
    freq = (index + half) % window - half
    phase = np.exp(-1j * np.pi * DEFOCUS * freq**2 / window)
    spread = dft.conj() @ (phase[:, None] * dft)
    near, far = spread[:half, :half], spread[:half, half:]
    stack = []
    for m in ((near + far) / 2, (near - far) / 2, dft[0::2, :half], dft[1::2, :half]):
        for form in (real_form(m), real_form(m).T):
            form = form.astype(np.float32)
            high = form.astype(ml_dtypes.bfloat16)
            low = (form - high.astype(np.float32)).astype(ml_dtypes.bfloat16)
            stack.append(np.concatenate([high, low], axis=1))
    return np.stack(stack)


PU, PU_T, PV, PV_T, FE, FE_T, FO, FO_T = range(8)


def split(x):
    high = x.astype(jnp.bfloat16)
    low = (x - high.astype(jnp.float32)).astype(jnp.bfloat16)
    return high, low


def dot(a, b):
    return jnp.dot(a, b, preferred_element_type=jnp.float32)


def from_left(w_ref, which, x):
    n = x.shape[0]
    high, low = split(x)
    wh, wl = w_ref[which, :, :n], w_ref[which, :, n:]
    return dot(wh, high) + dot(wh, low) + dot(wl, high)


def from_right(w_ref, which, x):
    n = x.shape[1]
    high, low = split(x)
    wh, wl = w_ref[which, :, :n], w_ref[which, :, n:]
    return dot(high, wh) + dot(low, wh) + dot(high, wl)


def rows(*parts):
    return jnp.concatenate(parts, axis=0)


def lanes(*parts):
    return jnp.concatenate(parts, axis=1)


def spread_field(w_ref, mats, xr, xi):
    u, v, ut, vt = mats
    h = xr.shape[0] // 2
    a = from_left(w_ref, u, rows(xr[:h] + xr[h:], xi[:h] + xi[h:]))
    b = from_left(w_ref, v, rows(xr[:h] - xr[h:], xi[:h] - xi[h:]))
    p, m = a + b, a - b
    yr, yi = rows(p[:h], m[:h]), rows(p[h:], m[h:])
    a = from_right(w_ref, ut, lanes(yr[:, :h] + yr[:, h:], yi[:, :h] + yi[:, h:]))
    b = from_right(w_ref, vt, lanes(yr[:, :h] - yr[:, h:], yi[:, :h] - yi[:, h:]))
    p, m = a + b, a - b
    return lanes(p[:, :h], m[:, :h]), lanes(p[:, h:], m[:, h:])


def to_far(w_ref, xr, xi):
    h = xr.shape[0] // 2
    e = from_left(w_ref, FE, rows(xr[:h] + xr[h:], xi[:h] + xi[h:]))
    o = from_left(w_ref, FO, rows(xr[:h] - xr[h:], xi[:h] - xi[h:]))
    yr, yi = rows(e[:h], o[:h]), rows(e[h:], o[h:])
    qe = from_right(w_ref, FE_T, lanes(yr[:, :h] + yr[:, h:], yi[:, :h] + yi[:, h:]))
    qo = from_right(w_ref, FO_T, lanes(yr[:, :h] - yr[:, h:], yi[:, :h] - yi[:, h:]))
    return qe, qo


def from_far(w_ref, ge, go):
    h = ge.shape[0] // 2
    a = from_right(w_ref, FE, ge)
    b = from_right(w_ref, FO, go)
    p, m = a + b, a - b
    yr, yi = lanes(p[:, :h], m[:, :h]), lanes(p[:, h:], m[:, h:])
    a = from_left(w_ref, FE_T, rows(yr[:h], yi[:h]))
    b = from_left(w_ref, FO_T, rows(yr[h:], yi[h:]))
    p, m = a + b, a - b
    return rows(p[:h], m[:h]), rows(p[h:], m[h:])


def one_hot(n, shift, across):
    a = lax.broadcasted_iota(jnp.int32, (n, n), 0)
    b = lax.broadcasted_iota(jnp.int32, (n, n), 1)
    gap = b - a - shift if across else a - b - shift
    return jnp.where((gap == 0) | (gap == -n), 1.0, 0.0).astype(jnp.bfloat16)


def take_left(m, x):
    high, low = split(x)
    return dot(m, high) + dot(m, low)


def take_right(x, m):
    high, low = split(x)
    return dot(high, m) + dot(low, m)


def move_probe(rs_ref, cs_ref, probe_ref, p_ref):
    n = probe_ref.shape[1]

    def one(s, carry):
        x = take_left(one_hot(n, lax.rem(rs_ref[s], n), False), lanes(probe_ref[0], probe_ref[1]))
        x = take_right(rows(x[:, :n], x[:, n:]), one_hot(n, lax.rem(cs_ref[s], n), True))
        p_ref[s, 0], p_ref[s, 1] = x[:n], x[n:]
        return carry

    for s in range(p_ref.shape[0]):
        one(s, 0)


def far_order(meas_ref, m_ref):
    slots, n = meas_ref.shape[0], meas_ref.shape[1]
    h = n // 2
    lane = lax.broadcasted_iota(jnp.int32, (n, h), 1)
    pick = lax.rem(lane, h // 2) * 2

    def one(s, carry):
        for par in range(2):
            got = [jnp.take_along_axis(meas_ref[s, :, k * h : (k + 1) * h], pick + par, axis=1) for k in range(2)]
            m_ref[s, par] = jnp.where(lane < h // 2, got[0], got[1])
        return carry

    lax.fori_loop(0, slots, one, 0)


def cut_windows(layer, rs_ref, cs_ref, ext_ref, t_ref):
    slots, n = t_ref.shape[1], t_ref.shape[3]
    h = n // 2
    step = n // 4

    def one(i, carry):
        at = pl.multiple_of(i * step, step)
        row = lax.broadcasted_iota(jnp.int32, (step, h), 0) + at
        lane = lax.broadcasted_iota(jnp.int32, (step, h), 1)
        for part in range(2):
            for k in range(2):
                blocks = [[ext_ref[layer, 2 * w + k, part, pl.ds(m * n + at, step), :] for m in range(3)] for w in range(2)]
                for s in range(slots):
                    r, c = rs_ref[s], cs_ref[s]
                    halves = [jnp.where(row >= r, e[0], jnp.where(row >= r - n, e[1], e[2])) for e in blocks]
                    t_ref[layer, s, part, pl.ds(at, step), k * h : (k + 1) * h] = jnp.where(lane + k * h >= c, halves[0], halves[1])
        return carry

    lax.fori_loop(0, n // step, one, 0)


def forward(w_ref, p_ref, t_ref, psi_ref):
    def one(s, carry):
        pr, pi = p_ref[s, 0], p_ref[s, 1]
        tr, ti = t_ref[0, s, 0], t_ref[0, s, 1]
        psi_ref[s, 0], psi_ref[s, 1] = spread_field(w_ref, (PU, PV, PU_T, PV_T), tr * pr - ti * pi, tr * pi + ti * pr)
        return carry

    for s in range(t_ref.shape[1]):
        one(s, 0)


def far_and_back(w_ref, live, m_ref, t_ref, psi_ref, q_ref, patch_ref):
    h = t_ref.shape[3] // 2

    def one(s, carry):
        xr, xi = psi_ref[s, 0], psi_ref[s, 1]
        tr, ti = t_ref[1, s, 0], t_ref[1, s, 1]
        far = to_far(w_ref, tr * xr - ti * xi, tr * xi + ti * xr)
        g = []
        for par, f in enumerate(far):
            fr, fi = f[:, :h], f[:, h:]
            inv = lax.rsqrt(jnp.maximum(fr * fr + fi * fi, FLOOR * FLOOR))
            amps = rows(*[m_ref[s, par, pl.ds(p, h, stride=2), :] for p in range(2)])
            weight = live[s] * (1.0 - amps * inv)
            g.append(lanes(weight * fr, weight * fi))
        br, bi = from_far(w_ref, *g)
        xr, xi = psi_ref[s, 0], psi_ref[s, 1]
        patch_ref[s, 0] = xr * br + xi * bi
        patch_ref[s, 1] = xr * bi - xi * br
        tr, ti = t_ref[1, s, 0], t_ref[1, s, 1]
        q_ref[s, 0] = tr * br + ti * bi
        q_ref[s, 1] = tr * bi - ti * br
        return carry

    for s in range(t_ref.shape[1]):
        one(s, 0)


def backward(w_ref, rs_ref, cs_ref, p_ref, t_ref, q_ref, patch_ref, pg_ref):
    n = t_ref.shape[3]
    pg_ref[...] = jnp.zeros_like(pg_ref)

    def one(s, carry):
        br, bi = spread_field(w_ref, (PU_T, PV_T, PU, PV), q_ref[s, 0], q_ref[s, 1])
        pr, pi = p_ref[s, 0], p_ref[s, 1]
        patch_ref[s, 0] = pr * br + pi * bi
        patch_ref[s, 1] = pr * bi - pi * br
        tr, ti = t_ref[0, s, 0], t_ref[0, s, 1]
        x = rows(tr * br + ti * bi, tr * bi - ti * br)
        x = take_right(x, one_hot(n, n - lax.rem(cs_ref[s], n), True))
        x = take_left(one_hot(n, n - lax.rem(rs_ref[s], n), False), lanes(x[:n], x[n:]))
        for part in range(2):
            pg_ref[part] += x[:, part * n : (part + 1) * n].reshape(pg_ref.shape[1:])
        return carry

    for s in range(t_ref.shape[1]):
        one(s, 0)


def add_patches(layer, rs_ref, cs_ref, patch_ref, gext_ref):
    slots, n = patch_ref.shape[0], patch_ref.shape[2]
    h = n // 2
    step = n // 8

    def one(i, carry):
        at = pl.multiple_of(i * step, step)
        row = lax.broadcasted_iota(jnp.int32, (step, h), 0) + at
        lane = lax.broadcasted_iota(jnp.int32, (step, h), 1)
        for part in range(2):
            for k in range(2):
                sums = [[None] * 3, [None] * 3]
                for s in range(slots):
                    r, c = rs_ref[s], cs_ref[s]
                    x = patch_ref[s, part, pl.ds(at, step), k * h : (k + 1) * h]
                    zero = jnp.zeros_like(x)
                    left = lane + k * h >= c
                    for w, y in enumerate((jnp.where(left, x, zero), jnp.where(left, zero, x))):
                        first, third = row >= r, row < r - n
                        parts = (jnp.where(first, y, zero), jnp.where(first | third, zero, y), jnp.where(third, y, zero))
                        for m in range(3):
                            sums[w][m] = parts[m] if sums[w][m] is None else sums[w][m] + parts[m]
                for w in range(2):
                    for m in range(3):
                        gext_ref[layer, 2 * w + k, part, pl.ds(m * n + at, step), :] = sums[w][m]
        return carry

    lax.fori_loop(0, n // step, one, 0)


MESH = pl.DeviceIdType.MESH
SIDES = ("up", "down", "left", "right")
OPPOSITE = {"up": "down", "down": "up", "left": "right", "right": "left"}


def step_kernel(scale, offsets_hbm, count_hbm, obj_hbm, probe_hbm, meas_hbm, w_hbm,
                grad_ref, total_ref,
                offsets_ref, count_ref, w_ref, probe_ref, meas_ref, ext_ref, gext_ref, t_ref, psi_ref, m_ref, q_ref, patch_ref, p_ref,
                corner_ref, side_ref, strip_ref, out_strip_ref,
                pg_ref, twin_ref, xs_ref, xr_ref, zs_ref, zr_ref, yr_ref, za_ref,
                local_sem, send_sem, recv_sem, sum_send, sum_recv):
    h = ext_ref.shape[4]
    tile = ext_ref.shape[3] - 2 * h
    row, col = lax.axis_index("row"), lax.axis_index("col")
    n_row, n_col = lax.axis_size("row"), lax.axis_size("col")
    near = {
        "up": (row > 0, {"row": row - 1, "col": col}),
        "down": (row < n_row - 1, {"row": row + 1, "col": col}),
        "left": (col > 0, {"row": row, "col": col - 1}),
        "right": (col < n_col - 1, {"row": row, "col": col + 1}),
    }
    y, x_hi = lax.rem(row, 4), lax.div(row, 4)
    core, z, x_lo = lax.rem(col, 2), lax.rem(lax.div(col, 2), 8), lax.div(col, 16)
    x = x_hi * 2 + x_lo
    twin = {"row": row, "col": col + 1 - 2 * core}

    def x_peer(k):
        other = lax.rem(x + k, 4)
        return {"row": lax.div(other, 2) * 4 + y, "col": lax.rem(other, 2) * 16 + z * 2 + core}

    def y_peer(k):
        return {"row": x_hi * 4 + lax.rem(y + k, 4), "col": col}

    def z_peer(k):
        return {"row": row, "col": x_lo * 16 + lax.rem(z + k, 8) * 2 + core}

    def send(number, src, dst, target, layer=None):
        sems = (sum_send.at[number], sum_recv.at[number]) if layer is None else (send_sem.at[layer, number], recv_sem.at[layer, number])
        return pltpu.make_async_remote_copy(src_ref=src, dst_ref=dst, send_sem=sems[0], recv_sem=sems[1], device_id=target, device_id_type=MESH)

    barrier = pltpu.get_barrier_semaphore()

    def greet(target):
        pl.semaphore_signal(barrier, inc=1, device_id=target, device_id_type=MESH)

    expected = 1 + 3 + 3 + 7
    for there, target in near.values():
        pl.when(there)(functools.partial(greet, target))
        expected = expected + jnp.where(there, 1, 0)
    for target in [twin] + [x_peer(k) for k in range(1, 4)] + [y_peer(k) for k in range(1, 4)] + [z_peer(k) for k in range(1, 8)]:
        greet(target)

    own = [pltpu.make_async_copy(meas_hbm, meas_ref, local_sem.at[0]),
           pltpu.make_async_copy(probe_hbm, probe_ref, local_sem.at[1]),
           pltpu.make_async_copy(w_hbm, w_ref, local_sem.at[2])]
    small = [pltpu.make_async_copy(offsets_hbm, offsets_ref, local_sem.at[7]), pltpu.make_async_copy(count_hbm, count_ref, local_sem.at[8])]
    for c in small:
        c.start()
    for layer in range(2):
        for b in range(2):
            own.append(pltpu.make_async_copy(obj_hbm.at[layer, :, :, pl.ds(b * h, h)], ext_ref.at[layer, 1 + b, :, pl.ds(h, tile), :], local_sem.at[3 + layer * 2 + b]))
    for c in own:
        c.start()
    got_own = set()

    def wait_own(i):
        if i not in got_own:
            got_own.add(i)
            own[i].wait()

    got = set()
    wait_own(0)
    far_order(meas_ref, m_ref)
    for c in small:
        c.wait()
    rs = [offsets_ref[0, 0, 0, i] - row * tile + h for i in range(4)]
    cs = [offsets_ref[0, 0, 1, i] - col * (2 * h) + h for i in range(4)]
    live = [jnp.where(i < count_ref[0, 0], 1.0, 0.0).astype(jnp.float32) for i in range(4)]
    wait_own(1)
    move_probe(rs, cs, probe_ref, p_ref)
    pl.semaphore_wait(barrier, expected)

    sums = []
    back = [{}, {}]
    low = (0, tile + h)
    halo = [{}, {}]
    begun = set()
    for layer in range(2):
        c = halo[layer]
        c[0] = "right", send(0, obj_hbm.at[layer, :, :, pl.ds(h, h)], ext_ref.at[layer, 0, :, pl.ds(h, tile), :], near["right"][1], layer)
        c[1] = "left", send(1, obj_hbm.at[layer, :, :, pl.ds(0, h)], ext_ref.at[layer, 3, :, pl.ds(h, tile), :], near["left"][1], layer)
        for b in range(2):
            c[2 + b] = "down", send(2 + b, obj_hbm.at[layer, :, pl.ds(tile - h, h), pl.ds(b * h, h)], ext_ref.at[layer, 1 + b, :, pl.ds(0, h), :], near["down"][1], layer)
            c[4 + b] = "up", send(4 + b, obj_hbm.at[layer, :, pl.ds(0, h), pl.ds(b * h, h)], ext_ref.at[layer, 1 + b, :, pl.ds(tile + h, h), :], near["up"][1], layer)
            for k in range(2):
                block = ext_ref.at[layer, 1 + b, :, pl.ds(low[k], h), :]
                side = ("left", "right")[b]
                c[6 + b * 2 + k] = side, send(6 + b * 2 + k, block, ext_ref.at[layer, (3, 0)[b], :, pl.ds(low[k], h), :], near[side][1], layer)

    def begin(layer, number, side, c):
        begun.add((layer, number))
        pl.when(near[side][0])(c.start)

    def start(layer, numbers):
        for number in numbers:
            begin(layer, number, *halo[layer][number])

    def forward_corners(layer):
        got.update((layer, i) for i in (2, 3, 4, 5))
        for b in range(2):
            for k in range(2):
                @pl.when(near[("up", "down")[k]][0])
                def _(b=b, k=k):
                    halo[layer][(2, 4)[k] + b][1].wait_recv()
                    start(layer, [6 + b * 2 + k])

    def halo_in(layer):
        got.update((layer, i) for i in (0, 1, 6, 7, 8, 9))
        wait_own(3 + layer * 2)
        wait_own(4 + layer * 2)
        for number in (0, 1, 6, 7, 8, 9):
            side, c = halo[layer][number]

            def arrive(side=side, c=c):
                pl.when(near[OPPOSITE[side]][0])(c.wait_recv)
            if number < 2:
                arrive()
            else:
                pl.when(near[("up", "down")[number % 2]][0])(arrive)

    start(0, (2, 3, 4, 5, 0, 1))
    forward_corners(0)
    wait_own(2)
    halo_in(0)
    start(1, (2, 3, 4, 5, 0, 1))
    cut_windows(0, rs, cs, ext_ref, t_ref)
    forward(w_ref, p_ref, t_ref, psi_ref)
    forward_corners(1)
    halo_in(1)
    cut_windows(1, rs, cs, ext_ref, t_ref)
    far_and_back(w_ref, live, m_ref, t_ref, psi_ref, q_ref, patch_ref)
    add_patches(1, rs, cs, patch_ref, gext_ref)

    back = [{}, {}]
    for layer in range(2):
        for b, side in enumerate(("left", "right")):
            for k in range(2):
                number = 10 + b * 2 + k
                back[layer][number] = side, send(number, gext_ref.at[layer, b * 3, :, pl.ds(low[k], h), :], corner_ref.at[layer, b, k], near[side][1], layer)
            back[layer][14 + b] = side, send(14 + b, gext_ref.at[layer, b * 3, :, pl.ds(h, tile), :], side_ref.at[layer, b], near[side][1], layer)
        for k, side in enumerate(("up", "down")):
            for b in range(2):
                number = 16 + k * 2 + b
                back[layer][number] = side, send(number, out_strip_ref.at[layer, k, b], strip_ref.at[layer, k, b], near[side][1], layer)

    def start_back(layer, numbers):
        for number in numbers:
            begin(layer, number, *back[layer][number])

    def strips_out(layer):
        got.update((layer, i) for i in (10, 11, 12, 13))
        for k in range(2):
            for b in range(2):
                out_strip_ref[layer, k, b] = gext_ref[layer, 1 + b, :, pl.ds(low[k], h), :]

                @pl.when(near[("left", "right")[b]][0])
                def _(k=k, b=b):
                    back[layer][10 + (1 - b) * 2 + k][1].wait_recv()
                    out_strip_ref[layer, k, b] += corner_ref[layer, 1 - b, k]
                start_back(layer, [16 + k * 2 + b])

    def join(layer):
        got.update((layer, i) for i in range(14, 20))
        for b in range(2):
            where = pl.ds(b * h, h)
            grad_ref[layer, :, :, where] = gext_ref[layer, 1 + b, :, pl.ds(h, tile), :]

            @pl.when(near[("left", "right")[b]][0])
            def _(b=b, where=where):
                back[layer][14 + 1 - b][1].wait_recv()
                grad_ref[layer, :, :, where] += side_ref[layer, 1 - b]

            @pl.when(near["down"][0])
            def _(b=b, where=where):
                back[layer][16 + b][1].wait_recv()
                grad_ref[layer, :, pl.ds(tile - h, h), where] += strip_ref[layer, 0, b]

            @pl.when(near["up"][0])
            def _(b=b, where=where):
                back[layer][18 + b][1].wait_recv()
                grad_ref[layer, :, pl.ds(0, h), where] += strip_ref[layer, 1, b]

    start_back(1, range(10, 16))
    backward(w_ref, rs, cs, p_ref, t_ref, q_ref, patch_ref, pg_ref)

    sums[:] = [send(0, pg_ref.at[1 - core], twin_ref, twin)]
    sums[0].start()
    strips_out(1)
    got.add(id(sums[0]))
    sums[0].wait_recv()
    xs_ref[...] = pg_ref[core] + twin_ref[...]

    def exchange(copies):
        for c in copies:
            c.start()
        sums.extend(copies)
        return copies

    def arrive(copies):
        for c in copies:
            got.add(id(c))
            c.wait_recv()

    along_x = exchange([send(k, xs_ref.at[lax.rem(x + k, 4)], xr_ref.at[k - 1], x_peer(k)) for k in range(1, 4)])
    add_patches(0, rs, cs, patch_ref, gext_ref)
    start_back(0, range(10, 14))
    arrive(along_x)
    zs_ref[...] = xs_ref[x] + xr_ref[0] + xr_ref[1] + xr_ref[2]
    along_z = exchange([send(3 + k, zs_ref.at[lax.rem(z + k, 8)], zr_ref.at[k - 1], z_peer(k)) for k in range(1, 8)])
    start_back(0, (14, 15))
    arrive(along_z)
    yr_ref[y] = zs_ref[z] + jnp.sum(zr_ref[...], axis=0)
    along_y = exchange([send(10 + k, yr_ref.at[y], yr_ref.at[y], y_peer(k)) for k in range(1, 4)])
    strips_out(0)
    arrive(along_y)
    za_ref[z] = (yr_ref[0] + yr_ref[1] + yr_ref[2] + yr_ref[3]) * scale
    along_z = exchange([send(13 + k, za_ref.at[z], za_ref.at[z], z_peer(k)) for k in range(1, 8)])
    arrive(along_z)
    total_ref[core, x] = za_ref[...]
    along_x = exchange([send(20 + k, za_ref, total_ref.at[core, x], x_peer(k)) for k in range(1, 4)])
    join(1)
    arrive(along_x)
    last = exchange([send(24, total_ref.at[core], total_ref.at[core], twin)])
    join(0)
    arrive(last)

    for i in range(7):
        wait_own(i)
    for c in sums:
        if id(c) not in got:
            c.wait_recv()
    for layer in range(2):
        for number, (side, c) in list(halo[layer].items()) + list(back[layer].items()):
            if (layer, number) in begun and (layer, number) not in got:
                def came(side=side, c=c):
                    pl.when(near[OPPOSITE[side]][0])(c.wait_recv)
                if 6 <= number < 10:
                    pl.when(near[("up", "down")[number % 2]][0])(came)
                else:
                    came()
    for c in sums:
        c.wait_send()
    for layer in range(2):
        pass
    for layer in range(2):
        for number, (side, c) in list(halo[layer].items()) + list(back[layer].items()):
            if (layer, number) not in begun:
                continue

            def sent(side=side, c=c):
                pl.when(near[side][0])(c.wait_send)
            if 6 <= number < 10:
                pl.when(near[("up", "down")[number % 2]][0])(sent)
            else:
                sent()


def step(scale, offsets, count, obj, probe, meas, w):
    layers, parts, tile, _ = obj.shape
    n = probe.shape[1]
    h = n // 2
    slots = meas.shape[0]
    vmem, hbm = (pl.BlockSpec(memory_space=s) for s in (pltpu.VMEM, pltpu.HBM))
    f32 = jnp.float32
    shapes = [
        probe.shape, meas.shape,
        (layers, 4, parts, tile + n, h), (layers, 4, parts, tile + n, h),
        (layers, slots, parts, n, n), (slots, parts, n, n), (slots, 2, n, h), (slots, parts, n, n),
        (slots, parts, n, n), (slots, parts, n, n),
        (layers, 2, 2, parts, h, h), (layers, 2, parts, tile, h), (layers, 2, 2, parts, h, h), (layers, 2, 2, parts, h, h),
        (2, 4, 8, 8, n), (4, 8, 8, n), (4, 8, 8, n), (3, 8, 8, n), (8, 8, n), (7, 8, n), (4, 8, n), (8, 8, n),
    ]
    dma = pltpu.SemaphoreType.DMA
    return pl.pallas_call(
        functools.partial(step_kernel, scale),
        out_shape=(jax.ShapeDtypeStruct(obj.shape, f32), jax.ShapeDtypeStruct((2, 4, 8, 8, n), f32)),
        in_specs=[hbm] * 6,
        out_specs=(vmem, vmem),
        scratch_shapes=[pltpu.SMEM(offsets.shape, jnp.int32), pltpu.SMEM(count.shape, jnp.int32), pltpu.VMEM(w.shape, w.dtype)] + [pltpu.VMEM(s, f32) for s in shapes]
        + [dma((9,)), dma((2, 20)), dma((2, 20)), dma((25,)), dma((25,))],
        compiler_params=pltpu.CompilerParams(collective_id=0, has_side_effects=True, vmem_limit_bytes=46 << 20),
        name="step",
    )(offsets, count, *(pltpu.with_memory_space_constraint(a, pltpu.HBM) for a in (obj, probe, meas, w)))


def local(w, object_slices, probe_field, scan_offsets, scan_count, measured):
    positions = lax.axis_size("row") * lax.axis_size("col") * measured.shape[2]
    scale = 1.0 / math.sqrt(positions)
    object_grad, total = step(scale, scan_offsets, scan_count, object_slices, probe_field, measured[0, 0], w)
    return object_grad, total.reshape(probe_field.shape)


def solution(mesh):
    placed = (
        P(None, None, "row", "col"),
        P(),
        P("row", "col", None, None),
        P("row", "col"),
        P("row", "col", None, None, None),
    )
    w = stage_matrices(256)
    return jax.shard_map(
        lambda *args: local(jnp.asarray(w), *args),
        mesh=mesh,
        in_specs=placed,
        out_specs=(P(None, None, "row", "col"), P()),
        check_vma=False,
    )
```

```python
import functools
import math

import jax
import jax.numpy as jnp
import ml_dtypes
import numpy as np
from jax import lax
from jax.experimental import pallas as pl
from jax.experimental.pallas import tpu as pltpu
from jax.sharding import PartitionSpec as P

DEFOCUS = 0.3
FLOOR = 0.5


def real_form(m):
    return np.block([[m.real, -m.imag], [m.imag, m.real]])


def stage_matrices(window):
    half = window // 2
    index = np.arange(window)
    dft = np.exp(-2j * np.pi * (index[:, None] * index[None, :] % window) / window) / math.sqrt(window)
    freq = (index + half) % window - half
    phase = np.exp(-1j * np.pi * DEFOCUS * freq**2 / window)
    spread = dft.conj() @ (phase[:, None] * dft)
    near, far = spread[:half, :half], spread[:half, half:]
    stack = []
    for m in ((near + far) / 2, (near - far) / 2, dft[0::2, :half], dft[1::2, :half]):
        for form in (real_form(m), real_form(m).T):
            form = form.astype(np.float32)
            high = form.astype(ml_dtypes.bfloat16)
            low = (form - high.astype(np.float32)).astype(ml_dtypes.bfloat16)
            stack.append(np.concatenate([high, low], axis=1))
    return np.stack(stack)


PU, PU_T, PV, PV_T, FE, FE_T, FO, FO_T = range(8)


def split(x):
    high = x.astype(jnp.bfloat16)
    low = (x - high.astype(jnp.float32)).astype(jnp.bfloat16)
    return high, low


def dot(a, b):
    return jnp.dot(a, b, preferred_element_type=jnp.float32)


def from_left(w_ref, which, x):
    n = x.shape[0]
    high, low = split(x)
    wh, wl = w_ref[which, :, :n], w_ref[which, :, n:]
    return dot(wh, high) + dot(wh, low) + dot(wl, high)


def from_right(w_ref, which, x):
    n = x.shape[1]
    high, low = split(x)
    wh, wl = w_ref[which, :, :n], w_ref[which, :, n:]
    return dot(high, wh) + dot(low, wh) + dot(high, wl)


def rows(*parts):
    return jnp.concatenate(parts, axis=0)


def lanes(*parts):
    return jnp.concatenate(parts, axis=1)


def spread_field(w_ref, mats, xr, xi):
    u, v, ut, vt = mats
    h = xr.shape[0] // 2
    a = from_left(w_ref, u, rows(xr[:h] + xr[h:], xi[:h] + xi[h:]))
    b = from_left(w_ref, v, rows(xr[:h] - xr[h:], xi[:h] - xi[h:]))
    p, m = a + b, a - b
    yr, yi = rows(p[:h], m[:h]), rows(p[h:], m[h:])
    a = from_right(w_ref, ut, lanes(yr[:, :h] + yr[:, h:], yi[:, :h] + yi[:, h:]))
    b = from_right(w_ref, vt, lanes(yr[:, :h] - yr[:, h:], yi[:, :h] - yi[:, h:]))
    p, m = a + b, a - b
    return lanes(p[:, :h], m[:, :h]), lanes(p[:, h:], m[:, h:])


def to_far(w_ref, xr, xi):
    h = xr.shape[0] // 2
    e = from_left(w_ref, FE, rows(xr[:h] + xr[h:], xi[:h] + xi[h:]))
    o = from_left(w_ref, FO, rows(xr[:h] - xr[h:], xi[:h] - xi[h:]))
    yr, yi = rows(e[:h], o[:h]), rows(e[h:], o[h:])
    qe = from_right(w_ref, FE_T, lanes(yr[:, :h] + yr[:, h:], yi[:, :h] + yi[:, h:]))
    qo = from_right(w_ref, FO_T, lanes(yr[:, :h] - yr[:, h:], yi[:, :h] - yi[:, h:]))
    return qe, qo


def from_far(w_ref, ge, go):
    h = ge.shape[0] // 2
    a = from_right(w_ref, FE, ge)
    b = from_right(w_ref, FO, go)
    p, m = a + b, a - b
    yr, yi = lanes(p[:, :h], m[:, :h]), lanes(p[:, h:], m[:, h:])
    a = from_left(w_ref, FE_T, rows(yr[:h], yi[:h]))
    b = from_left(w_ref, FO_T, rows(yr[h:], yi[h:]))
    p, m = a + b, a - b
    return rows(p[:h], m[:h]), rows(p[h:], m[h:])


def one_hot(n, shift, across):
    a = lax.broadcasted_iota(jnp.int32, (n, n), 0)
    b = lax.broadcasted_iota(jnp.int32, (n, n), 1)
    gap = b - a - shift if across else a - b - shift
    return jnp.where((gap == 0) | (gap == -n), 1.0, 0.0).astype(jnp.bfloat16)


def take_left(m, x):
    high, low = split(x)
    return dot(m, high) + dot(m, low)


def take_right(x, m):
    high, low = split(x)
    return dot(high, m) + dot(low, m)


def move_probe(rs_ref, cs_ref, probe_ref, p_ref):
    n = probe_ref.shape[1]

    def one(s, carry):
        x = take_left(one_hot(n, lax.rem(rs_ref[s], n), False), lanes(probe_ref[0], probe_ref[1]))
        x = take_right(rows(x[:, :n], x[:, n:]), one_hot(n, lax.rem(cs_ref[s], n), True))
        p_ref[s, 0], p_ref[s, 1] = x[:n], x[n:]
        return carry

    for s in range(p_ref.shape[0]):
        one(s, 0)


def far_order(meas_ref, m_ref):
    slots, n = meas_ref.shape[0], meas_ref.shape[1]
    h = n // 2
    lane = lax.broadcasted_iota(jnp.int32, (n, h), 1)
    pick = lax.rem(lane, h // 2) * 2

    def one(s, carry):
        for par in range(2):
            got = [jnp.take_along_axis(meas_ref[s, :, k * h : (k + 1) * h], pick + par, axis=1) for k in range(2)]
            m_ref[s, par] = jnp.where(lane < h // 2, got[0], got[1])
        return carry

    lax.fori_loop(0, slots, one, 0)


def cut_windows(layer, rs_ref, cs_ref, ext_ref, t_ref):
    slots, n = t_ref.shape[1], t_ref.shape[3]
    h = n // 2
    step = n // 4

    def one(i, carry):
        at = pl.multiple_of(i * step, step)
        row = lax.broadcasted_iota(jnp.int32, (step, h), 0) + at
        lane = lax.broadcasted_iota(jnp.int32, (step, h), 1)
        for part in range(2):
            for k in range(2):
                blocks = [[ext_ref[layer, 2 * w + k, part, pl.ds(m * n + at, step), :] for m in range(3)] for w in range(2)]
                for s in range(slots):
                    r, c = rs_ref[s], cs_ref[s]
                    halves = [jnp.where(row >= r, e[0], jnp.where(row >= r - n, e[1], e[2])) for e in blocks]
                    t_ref[layer, s, part, pl.ds(at, step), k * h : (k + 1) * h] = jnp.where(lane + k * h >= c, halves[0], halves[1])
        return carry

    lax.fori_loop(0, n // step, one, 0)


def forward(w_ref, p_ref, t_ref, psi_ref):
    def one(s, carry):
        pr, pi = p_ref[s, 0], p_ref[s, 1]
        tr, ti = t_ref[0, s, 0], t_ref[0, s, 1]
        psi_ref[s, 0], psi_ref[s, 1] = spread_field(w_ref, (PU, PV, PU_T, PV_T), tr * pr - ti * pi, tr * pi + ti * pr)
        return carry

    for s in range(t_ref.shape[1]):
        one(s, 0)


def far_and_back(w_ref, live, m_ref, t_ref, psi_ref, q_ref, patch_ref):
    h = t_ref.shape[3] // 2

    def one(s, carry):
        xr, xi = psi_ref[s, 0], psi_ref[s, 1]
        tr, ti = t_ref[1, s, 0], t_ref[1, s, 1]
        far = to_far(w_ref, tr * xr - ti * xi, tr * xi + ti * xr)
        g = []
        for par, f in enumerate(far):
            fr, fi = f[:, :h], f[:, h:]
            inv = lax.rsqrt(jnp.maximum(fr * fr + fi * fi, FLOOR * FLOOR))
            amps = rows(*[m_ref[s, par, pl.ds(p, h, stride=2), :] for p in range(2)])
            weight = live[s] * (1.0 - amps * inv)
            g.append(lanes(weight * fr, weight * fi))
        br, bi = from_far(w_ref, *g)
        xr, xi = psi_ref[s, 0], psi_ref[s, 1]
        patch_ref[s, 0] = xr * br + xi * bi
        patch_ref[s, 1] = xr * bi - xi * br
        tr, ti = t_ref[1, s, 0], t_ref[1, s, 1]
        q_ref[s, 0] = tr * br + ti * bi
        q_ref[s, 1] = tr * bi - ti * br
        return carry

    for s in range(t_ref.shape[1]):
        one(s, 0)


def backward(w_ref, rs_ref, cs_ref, p_ref, t_ref, q_ref, patch_ref, pg_ref):
    n = t_ref.shape[3]
    pg_ref[...] = jnp.zeros_like(pg_ref)

    def one(s, carry):
        br, bi = spread_field(w_ref, (PU_T, PV_T, PU, PV), q_ref[s, 0], q_ref[s, 1])
        pr, pi = p_ref[s, 0], p_ref[s, 1]
        patch_ref[s, 0] = pr * br + pi * bi
        patch_ref[s, 1] = pr * bi - pi * br
        tr, ti = t_ref[0, s, 0], t_ref[0, s, 1]
        x = rows(tr * br + ti * bi, tr * bi - ti * br)
        x = take_right(x, one_hot(n, n - lax.rem(cs_ref[s], n), True))
        x = take_left(one_hot(n, n - lax.rem(rs_ref[s], n), False), lanes(x[:n], x[n:]))
        for part in range(2):
            pg_ref[part] += x[:, part * n : (part + 1) * n].reshape(pg_ref.shape[1:])
        return carry

    for s in range(t_ref.shape[1]):
        one(s, 0)


def add_patches(layer, rs_ref, cs_ref, patch_ref, gext_ref):
    slots, n = patch_ref.shape[0], patch_ref.shape[2]
    h = n // 2
    step = n // 8

    def one(i, carry):
        at = pl.multiple_of(i * step, step)
        row = lax.broadcasted_iota(jnp.int32, (step, h), 0) + at
        lane = lax.broadcasted_iota(jnp.int32, (step, h), 1)
        for part in range(2):
            for k in range(2):
                sums = [[None] * 3, [None] * 3]
                for s in range(slots):
                    r, c = rs_ref[s], cs_ref[s]
                    x = patch_ref[s, part, pl.ds(at, step), k * h : (k + 1) * h]
                    zero = jnp.zeros_like(x)
                    left = lane + k * h >= c
                    for w, y in enumerate((jnp.where(left, x, zero), jnp.where(left, zero, x))):
                        first, third = row >= r, row < r - n
                        parts = (jnp.where(first, y, zero), jnp.where(first | third, zero, y), jnp.where(third, y, zero))
                        for m in range(3):
                            sums[w][m] = parts[m] if sums[w][m] is None else sums[w][m] + parts[m]
                for w in range(2):
                    for m in range(3):
                        gext_ref[layer, 2 * w + k, part, pl.ds(m * n + at, step), :] = sums[w][m]
        return carry

    lax.fori_loop(0, n // step, one, 0)


MESH = pl.DeviceIdType.MESH
SIDES = ("up", "down", "left", "right")
OPPOSITE = {"up": "down", "down": "up", "left": "right", "right": "left"}


def step_kernel(scale, offsets_hbm, count_hbm, obj_hbm, probe_hbm, meas_hbm, w_hbm,
                grad_ref, total_ref,
                offsets_ref, count_ref, w_ref, probe_ref, meas_ref, ext_ref, gext_ref, t_ref, psi_ref, m_ref, q_ref, patch_ref, p_ref,
                corner_ref, side_ref, strip_ref, out_strip_ref,
                pg_ref, twin_ref, xs_ref, xr_ref, zs_ref, zr_ref, yr_ref, za_ref,
                local_sem, send_sem, recv_sem, sum_send, sum_recv):
    h = ext_ref.shape[4]
    tile = ext_ref.shape[3] - 2 * h
    row, col = lax.axis_index("row"), lax.axis_index("col")
    n_row, n_col = lax.axis_size("row"), lax.axis_size("col")
    near = {
        "up": (row > 0, {"row": row - 1, "col": col}),
        "down": (row < n_row - 1, {"row": row + 1, "col": col}),
        "left": (col > 0, {"row": row, "col": col - 1}),
        "right": (col < n_col - 1, {"row": row, "col": col + 1}),
    }
    y, x_hi = lax.rem(row, 4), lax.div(row, 4)
    core, z, x_lo = lax.rem(col, 2), lax.rem(lax.div(col, 2), 8), lax.div(col, 16)
    x = x_hi * 2 + x_lo
    twin = {"row": row, "col": col + 1 - 2 * core}

    def x_peer(k):
        other = lax.rem(x + k, 4)
        return {"row": lax.div(other, 2) * 4 + y, "col": lax.rem(other, 2) * 16 + z * 2 + core}

    def y_peer(k):
        return {"row": x_hi * 4 + lax.rem(y + k, 4), "col": col}

    def z_peer(k):
        return {"row": row, "col": x_lo * 16 + lax.rem(z + k, 8) * 2 + core}

    def send(number, src, dst, target, layer=None):
        sems = (sum_send.at[number], sum_recv.at[number]) if layer is None else (send_sem.at[layer, number], recv_sem.at[layer, number])
        return pltpu.make_async_remote_copy(src_ref=src, dst_ref=dst, send_sem=sems[0], recv_sem=sems[1], device_id=target, device_id_type=MESH)

    barrier = pltpu.get_barrier_semaphore()

    def greet(target):
        pl.semaphore_signal(barrier, inc=1, device_id=target, device_id_type=MESH)

    expected = 1 + 3 + 3 + 7
    for there, target in near.values():
        pl.when(there)(functools.partial(greet, target))
        expected = expected + jnp.where(there, 1, 0)
    for target in [twin] + [x_peer(k) for k in range(1, 4)] + [y_peer(k) for k in range(1, 4)] + [z_peer(k) for k in range(1, 8)]:
        greet(target)

    own = [pltpu.make_async_copy(meas_hbm, meas_ref, local_sem.at[0]),
           pltpu.make_async_copy(probe_hbm, probe_ref, local_sem.at[1]),
           pltpu.make_async_copy(w_hbm, w_ref, local_sem.at[2])]
    small = [pltpu.make_async_copy(offsets_hbm, offsets_ref, local_sem.at[7]), pltpu.make_async_copy(count_hbm, count_ref, local_sem.at[8])]
    for c in small:
        c.start()
    for layer in range(2):
        for b in range(2):
            own.append(pltpu.make_async_copy(obj_hbm.at[layer, :, :, pl.ds(b * h, h)], ext_ref.at[layer, 1 + b, :, pl.ds(h, tile), :], local_sem.at[3 + layer * 2 + b]))
    for c in own:
        c.start()
    got_own = set()

    def wait_own(i):
        if i not in got_own:
            got_own.add(i)
            own[i].wait()

    got = set()
    wait_own(0)
    far_order(meas_ref, m_ref)
    for c in small:
        c.wait()
    rs = [offsets_ref[0, 0, 0, i] - row * tile + h for i in range(4)]
    cs = [offsets_ref[0, 0, 1, i] - col * (2 * h) + h for i in range(4)]
    live = [jnp.where(i < count_ref[0, 0], 1.0, 0.0).astype(jnp.float32) for i in range(4)]
    wait_own(1)
    move_probe(rs, cs, probe_ref, p_ref)
    pl.semaphore_wait(barrier, expected)

    sums = []
    back = [{}, {}]
    low = (0, tile + h)
    halo = [{}, {}]
    begun = set()
    for layer in range(2):
        c = halo[layer]
        c[0] = "right", send(0, obj_hbm.at[layer, :, :, pl.ds(h, h)], ext_ref.at[layer, 0, :, pl.ds(h, tile), :], near["right"][1], layer)
        c[1] = "left", send(1, obj_hbm.at[layer, :, :, pl.ds(0, h)], ext_ref.at[layer, 3, :, pl.ds(h, tile), :], near["left"][1], layer)
        for b in range(2):
            c[2 + b] = "down", send(2 + b, obj_hbm.at[layer, :, pl.ds(tile - h, h), pl.ds(b * h, h)], ext_ref.at[layer, 1 + b, :, pl.ds(0, h), :], near["down"][1], layer)
            c[4 + b] = "up", send(4 + b, obj_hbm.at[layer, :, pl.ds(0, h), pl.ds(b * h, h)], ext_ref.at[layer, 1 + b, :, pl.ds(tile + h, h), :], near["up"][1], layer)
            for k in range(2):
                block = ext_ref.at[layer, 1 + b, :, pl.ds(low[k], h), :]
                side = ("left", "right")[b]
                c[6 + b * 2 + k] = side, send(6 + b * 2 + k, block, ext_ref.at[layer, (3, 0)[b], :, pl.ds(low[k], h), :], near[side][1], layer)

    def begin(layer, number, side, c):
        begun.add((layer, number))
        pl.when(near[side][0])(c.start)

    def start(layer, numbers):
        for number in numbers:
            begin(layer, number, *halo[layer][number])

    def forward_corners(layer):
        got.update((layer, i) for i in (2, 3, 4, 5))
        for b in range(2):
            for k in range(2):
                @pl.when(near[("up", "down")[k]][0])
                def _(b=b, k=k):
                    halo[layer][(2, 4)[k] + b][1].wait_recv()
                    start(layer, [6 + b * 2 + k])

    def halo_in(layer):
        got.update((layer, i) for i in (0, 1, 6, 7, 8, 9))
        wait_own(3 + layer * 2)
        wait_own(4 + layer * 2)
        for number in (0, 1, 6, 7, 8, 9):
            side, c = halo[layer][number]

            def arrive(side=side, c=c):
                pl.when(near[OPPOSITE[side]][0])(c.wait_recv)
            if number < 2:
                arrive()
            else:
                pl.when(near[("up", "down")[number % 2]][0])(arrive)

    start(0, (2, 3, 4, 5, 0, 1))
    forward_corners(0)
    wait_own(2)
    halo_in(0)
    start(1, (2, 3, 4, 5, 0, 1))
    cut_windows(0, rs, cs, ext_ref, t_ref)
    forward(w_ref, p_ref, t_ref, psi_ref)
    forward_corners(1)
    halo_in(1)
    cut_windows(1, rs, cs, ext_ref, t_ref)
    far_and_back(w_ref, live, m_ref, t_ref, psi_ref, q_ref, patch_ref)
    add_patches(1, rs, cs, patch_ref, gext_ref)

    back = [{}, {}]
    for layer in range(2):
        for b, side in enumerate(("left", "right")):
            for k in range(2):
                number = 10 + b * 2 + k
                back[layer][number] = side, send(number, gext_ref.at[layer, b * 3, :, pl.ds(low[k], h), :], corner_ref.at[layer, b, k], near[side][1], layer)
            back[layer][14 + b] = side, send(14 + b, gext_ref.at[layer, b * 3, :, pl.ds(h, tile), :], side_ref.at[layer, b], near[side][1], layer)
        for k, side in enumerate(("up", "down")):
            for b in range(2):
                number = 16 + k * 2 + b
                back[layer][number] = side, send(number, out_strip_ref.at[layer, k, b], strip_ref.at[layer, k, b], near[side][1], layer)

    def start_back(layer, numbers):
        for number in numbers:
            begin(layer, number, *back[layer][number])

    def strips_out(layer):
        got.update((layer, i) for i in (10, 11, 12, 13))
        for k in range(2):
            for b in range(2):
                out_strip_ref[layer, k, b] = gext_ref[layer, 1 + b, :, pl.ds(low[k], h), :]

                @pl.when(near[("left", "right")[b]][0])
                def _(k=k, b=b):
                    back[layer][10 + (1 - b) * 2 + k][1].wait_recv()
                    out_strip_ref[layer, k, b] += corner_ref[layer, 1 - b, k]
                start_back(layer, [16 + k * 2 + b])

    def join(layer):
        got.update((layer, i) for i in range(14, 20))
        for b in range(2):
            where = pl.ds(b * h, h)
            grad_ref[layer, :, :, where] = gext_ref[layer, 1 + b, :, pl.ds(h, tile), :]

            @pl.when(near[("left", "right")[b]][0])
            def _(b=b, where=where):
                back[layer][14 + 1 - b][1].wait_recv()
                grad_ref[layer, :, :, where] += side_ref[layer, 1 - b]

            @pl.when(near["down"][0])
            def _(b=b, where=where):
                back[layer][16 + b][1].wait_recv()
                grad_ref[layer, :, pl.ds(tile - h, h), where] += strip_ref[layer, 0, b]

            @pl.when(near["up"][0])
            def _(b=b, where=where):
                back[layer][18 + b][1].wait_recv()
                grad_ref[layer, :, pl.ds(0, h), where] += strip_ref[layer, 1, b]

    start_back(1, range(10, 16))
    backward(w_ref, rs, cs, p_ref, t_ref, q_ref, patch_ref, pg_ref)

    sums[:] = [send(0, pg_ref.at[1 - core], twin_ref, twin)]
    sums[0].start()
    strips_out(1)
    got.add(id(sums[0]))
    sums[0].wait_recv()
    xs_ref[...] = pg_ref[core] + twin_ref[...]

    def exchange(copies):
        for c in copies:
            c.start()
        sums.extend(copies)
        return copies

    def arrive(copies):
        for c in copies:
            got.add(id(c))
            c.wait_recv()

    along_x = exchange([send(k, xs_ref.at[lax.rem(x + k, 4)], xr_ref.at[k - 1], x_peer(k)) for k in range(1, 4)])
    add_patches(0, rs, cs, patch_ref, gext_ref)
    start_back(0, range(10, 14))
    arrive(along_x)
    zs_ref[...] = xs_ref[x] + xr_ref[0] + xr_ref[1] + xr_ref[2]
    along_z = exchange([send(3 + k, zs_ref.at[lax.rem(z + k, 8)], zr_ref.at[k - 1], z_peer(k)) for k in range(1, 8)])
    arrive(along_z)
    yr_ref[y] = zs_ref[z] + jnp.sum(zr_ref[...], axis=0)
    along_y = exchange([send(10 + k, yr_ref.at[y], yr_ref.at[y], y_peer(k)) for k in range(1, 4)])
    start_back(0, (14, 15))
    strips_out(0)
    arrive(along_y)
    za_ref[z] = (yr_ref[0] + yr_ref[1] + yr_ref[2] + yr_ref[3]) * scale
    along_z = exchange([send(13 + k, za_ref.at[z], za_ref.at[z], z_peer(k)) for k in range(1, 8)])
    arrive(along_z)
    total_ref[core, x] = za_ref[...]
    along_x = exchange([send(20 + k, za_ref, total_ref.at[core, x], x_peer(k)) for k in range(1, 4)])
    join(1)
    arrive(along_x)
    last = exchange([send(24, total_ref.at[core], total_ref.at[core], twin)])
    join(0)
    arrive(last)

    for i in range(7):
        wait_own(i)
    for c in sums:
        if id(c) not in got:
            c.wait_recv()
    for layer in range(2):
        for number, (side, c) in list(halo[layer].items()) + list(back[layer].items()):
            if (layer, number) in begun and (layer, number) not in got:
                def came(side=side, c=c):
                    pl.when(near[OPPOSITE[side]][0])(c.wait_recv)
                if 6 <= number < 10:
                    pl.when(near[("up", "down")[number % 2]][0])(came)
                else:
                    came()
    for c in sums:
        c.wait_send()
    for layer in range(2):
        pass
    for layer in range(2):
        for number, (side, c) in list(halo[layer].items()) + list(back[layer].items()):
            if (layer, number) not in begun:
                continue

            def sent(side=side, c=c):
                pl.when(near[side][0])(c.wait_send)
            if 6 <= number < 10:
                pl.when(near[("up", "down")[number % 2]][0])(sent)
            else:
                sent()


def step(scale, offsets, count, obj, probe, meas, w):
    layers, parts, tile, _ = obj.shape
    n = probe.shape[1]
    h = n // 2
    slots = meas.shape[0]
    vmem, hbm = (pl.BlockSpec(memory_space=s) for s in (pltpu.VMEM, pltpu.HBM))
    f32 = jnp.float32
    shapes = [
        probe.shape, meas.shape,
        (layers, 4, parts, tile + n, h), (layers, 4, parts, tile + n, h),
        (layers, slots, parts, n, n), (slots, parts, n, n), (slots, 2, n, h), (slots, parts, n, n),
        (slots, parts, n, n), (slots, parts, n, n),
        (layers, 2, 2, parts, h, h), (layers, 2, parts, tile, h), (layers, 2, 2, parts, h, h), (layers, 2, 2, parts, h, h),
        (2, 4, 8, 8, n), (4, 8, 8, n), (4, 8, 8, n), (3, 8, 8, n), (8, 8, n), (7, 8, n), (4, 8, n), (8, 8, n),
    ]
    dma = pltpu.SemaphoreType.DMA
    return pl.pallas_call(
        functools.partial(step_kernel, scale),
        out_shape=(jax.ShapeDtypeStruct(obj.shape, f32), jax.ShapeDtypeStruct((2, 4, 8, 8, n), f32)),
        in_specs=[hbm] * 6,
        out_specs=(vmem, vmem),
        scratch_shapes=[pltpu.SMEM(offsets.shape, jnp.int32), pltpu.SMEM(count.shape, jnp.int32), pltpu.VMEM(w.shape, w.dtype)] + [pltpu.VMEM(s, f32) for s in shapes]
        + [dma((9,)), dma((2, 20)), dma((2, 20)), dma((25,)), dma((25,))],
        compiler_params=pltpu.CompilerParams(collective_id=0, has_side_effects=True, vmem_limit_bytes=46 << 20),
        name="step",
    )(offsets, count, *(pltpu.with_memory_space_constraint(a, pltpu.HBM) for a in (obj, probe, meas, w)))


def local(w, object_slices, probe_field, scan_offsets, scan_count, measured):
    positions = lax.axis_size("row") * lax.axis_size("col") * measured.shape[2]
    scale = 1.0 / math.sqrt(positions)
    object_grad, total = step(scale, scan_offsets, scan_count, object_slices, probe_field, measured[0, 0], w)
    return object_grad, total.reshape(probe_field.shape)


def solution(mesh):
    placed = (
        P(None, None, "row", "col"),
        P(),
        P("row", "col", None, None),
        P("row", "col"),
        P("row", "col", None, None, None),
    )
    w = stage_matrices(256)
    return jax.shard_map(
        lambda *args: local(jnp.asarray(w), *args),
        mesh=mesh,
        in_specs=placed,
        out_specs=(P(None, None, "row", "col"), P()),
        check_vma=False,
    )
```
